32 devices in a mesh: ctx: 8 (over z, y), head: 4 (over x, core).
Axes of the slice: x: 2, y: 2, z: 4, core: 2. Of those that a mesh axis runs over, the one named last changes fastest.
Arguments:
- queries: bfloat16 [4096, 32, 128], P(('ctx', 'head')), may hold values from -6 to 6
- key_states: bfloat16 [4096, 4, 128], P(('ctx', 'head')), may hold values from -6 to 6
- value_states: bfloat16 [4096, 4, 128], P(('ctx', 'head')), may hold values from -6 to 6
- out_grad: bfloat16 [4096, 32, 128], P(('ctx', 'head')), may hold values from -6 to 6
- log_sums: float32 [32, 4096], P('head', 'ctx'), may hold values from 3 to 6
- row_deltas: float32 [32, 4096], P('head', 'ctx'), may hold values from -10 to 10
- block_pairs: int32 [64, 4], replicated, may hold values from 0 to 63, as said below
- pair_kinds: int32 [64, 4], replicated, may hold values from 0 to 2, as said below
Outputs:
- query_grad: bfloat16 [4096, 32, 128], P(('ctx', 'head'))
- key_grad: bfloat16 [4096, 4, 128], P(('ctx', 'head'))
- value_grad: bfloat16 [4096, 4, 128], P(('ctx', 'head'))
The draws below stay inside these ranges and needn't reach their ends.
Inputs may be any that keep to these rules, and one draw needn't show every extreme that they name: `block_pairs`: row g lists the key blocks of query block g. Slot 0 names g itself, slot 1 names g - 1, slot 2 names key block 0; slots 3 and up name blocks of shards at least two shards before the shard of g, never of shard 0. The blocks of the live slots of a row are distinct and none is later than g; a slot of kind 0 names block 0. Counting shards of 8 consecutive query blocks, the query blocks of one shard name at most one key block held by any other single shard, and this is reached. `pair_kinds`: 1 marks a full block pair, 2 the pair of a block with itself, 0 an unused slot. Slot 0 is always 2 and no other slot is 2; slot 1 is 0 only for g = 0; slot 2 is 0 exactly for g < 2 and for the query blocks of the second shard.
All inputs are finite; a program needn't handle non-finite values.
Results may differ from the reference program's by a relative error of at most 0.0012.
The reference program's roundings to bfloat16 on the way count: a program that leaves them out, or rounds other values in their place, can miss the bound.
Values may be sent and summed in bfloat16 or wider, within the bound.
A program may use at most 64 MiB of HBM per device.

```python
import jax
import jax.numpy as jnp
from jax import lax

HD = 128
QH = 32
KVH = 4
BLOCK = 64
REMOTE = 1
TOKENS = 4096
QB_DEV = 8
NQB = 64


def pair_table(key):
    base_key = jax.random.fold_in(key, 4711)
    shards = NQB // QB_DEV
    spread = QB_DEV * REMOTE
    pool = max(spread, shards)
    order_keys = jax.random.split(jax.random.fold_in(base_key, 1), shards)
    orders = jax.vmap(lambda sub_key: jax.random.permutation(sub_key, pool)[:spread])(order_keys).astype(jnp.int32)
    links = jax.random.randint(jax.random.fold_in(base_key, 2), (shards, shards), 0, QB_DEV).astype(jnp.int32)
    dropped = jax.random.randint(jax.random.fold_in(base_key, 3), (shards, spread), 0, 4)
    shard_ids = jnp.arange(shards, dtype=jnp.int32)[:, None]
    owners = jnp.minimum(orders, shards - 1).astype(jnp.int32)
    is_live = (orders >= 1) & (orders <= shard_ids - 2) & (dropped > 0)
    chosen = jnp.take_along_axis(links, owners, axis=1)
    far_blocks = jnp.where(is_live, owners * QB_DEV + chosen, 0).astype(jnp.int32).reshape(NQB, REMOTE)
    far_kinds = is_live.astype(jnp.int32).reshape(NQB, REMOTE)
    query_ids = jnp.arange(NQB, dtype=jnp.int32)
    shard_of = query_ids // QB_DEV
    prev_kind = (query_ids >= 1).astype(jnp.int32)
    hub_kind = ((query_ids >= 2) & (shard_of != 1)).astype(jnp.int32)
    near_blocks = jnp.stack([query_ids, jnp.where(prev_kind > 0, query_ids - 1, 0), jnp.zeros_like(query_ids)], axis=1)
    near_kinds = jnp.stack([jnp.full_like(query_ids, 2), prev_kind, hub_kind], axis=1)
    blocks_all = jnp.concatenate([near_blocks, far_blocks], axis=1).astype(jnp.int32)
    kinds_all = jnp.concatenate([near_kinds, far_kinds], axis=1).astype(jnp.int32)
    return (blocks_all, kinds_all)


def draw_block_pairs(key, part):
    return pair_table(key)[0]


def draw_pair_kinds(key, part):
    return pair_table(key)[1]


def block_levels(own_key, shape, cuts, smallest, top_value):
    level = 1.0
    for position, parts in cuts:
        draws = jax.random.uniform(jax.random.fold_in(jax.random.fold_in(own_key, 6), position), (parts,), jnp.float32, smallest / len(cuts), top_value / len(cuts))
        level = level * jnp.repeat(jnp.exp(draws), shape[position] // parts).reshape((-1,) + (1,) * (len(shape) - 1 - position))
    return level


def bell_draw(stream_key, extent, width, limit, cuts=(), held_as=jnp.bfloat16):
    result = width * jax.random.normal(stream_key, extent, jnp.float32)
    if cuts:
        result = result * block_levels(stream_key, extent, cuts, -0.22, 0.18)
    return jnp.clip(result, -limit, limit).astype(held_as)


def setup_inputs(seed: int = 0) -> dict:
    key_list = jax.random.split(jax.random.key(seed), 9)
    queries = bell_draw(key_list[0], (TOKENS, QH, HD), 1.0, 6.0, ((0, 32),))
    key_states = bell_draw(key_list[1], (TOKENS, KVH, HD), 1.0, 6.0, ((0, 32),))
    value_states = bell_draw(key_list[2], (TOKENS, KVH, HD), 1.0, 6.0, ((0, 32),))
    out_grad = bell_draw(key_list[3], (TOKENS, QH, HD), 1.0, 6.0, ((0, 32),))
    log_sums = jnp.clip(3.0 + 3.0 * jax.random.uniform(key_list[4], (QH, TOKENS), jnp.float32) ** block_levels(key_list[4], (QH, TOKENS), ((0, 4), (1, 8)), -0.2, 0.2), 3.0, 6.0)
    row_deltas = bell_draw(key_list[5], (QH, TOKENS), 2.0, 10.0, ((0, 4), (1, 8)), jnp.float32)
    block_pairs = draw_block_pairs(jax.random.fold_in(key_list[8], 71), 0)
    pair_kinds = draw_pair_kinds(jax.random.fold_in(key_list[8], 71), 0)
    return {"queries": queries, "key_states": key_states, "value_states": value_states, "out_grad": out_grad, "log_sums": log_sums, "row_deltas": row_deltas, "block_pairs": block_pairs, "pair_kinds": pair_kinds}


def reference(queries, key_states, value_states, out_grad, log_sums, row_deltas, block_pairs, pair_kinds):
    head_group = QH // KVH
    score_scale = HD ** -0.5
    causal = jnp.arange(BLOCK)[:, None] >= jnp.arange(BLOCK)[None, :]
    query_all = queries.astype(jnp.float32).reshape(NQB, BLOCK, KVH, head_group, HD).transpose(2, 0, 1, 3, 4)
    grad_all = out_grad.astype(jnp.float32).reshape(NQB, BLOCK, KVH, head_group, HD).transpose(2, 0, 1, 3, 4)
    key_all = key_states.astype(jnp.float32).reshape(NQB, BLOCK, KVH, HD).transpose(2, 0, 1, 3)
    value_all = value_states.astype(jnp.float32).reshape(NQB, BLOCK, KVH, HD).transpose(2, 0, 1, 3)
    log_all = log_sums.reshape(KVH, head_group, NQB, BLOCK).transpose(0, 2, 1, 3)
    delta_all = row_deltas.reshape(KVH, head_group, NQB, BLOCK).transpose(0, 2, 1, 3)

    def per_head(inputs):
        head_queries, head_grads, head_keys, head_values, head_logs, head_deltas = inputs

        def per_slot(running, column):
            query_acc, key_acc, value_acc = running
            slot_blocks, slot_kinds = column
            key_tile = head_keys[slot_blocks]
            value_tile = head_values[slot_blocks]
            scores = jnp.einsum("nbgd,nkd->ngbk", head_queries, key_tile) * score_scale
            weights = jnp.exp(scores - head_logs[..., None])
            full_pair = (slot_kinds == 1)[:, None, None, None]
            diagonal_pair = (slot_kinds == 2)[:, None, None, None]
            weights = jnp.where(full_pair | (diagonal_pair & causal), weights, 0.0)
            rounded = lax.optimization_barrier(weights.astype(jnp.bfloat16)).astype(jnp.float32)
            value_term = jnp.einsum("ngbk,nbgd->nkd", rounded, head_grads)
            prob_grad = jnp.einsum("nbgd,nkd->ngbk", head_grads, value_tile)
            dscore = weights * (prob_grad - head_deltas[..., None])
            dscore = lax.optimization_barrier(dscore.astype(jnp.bfloat16)).astype(jnp.float32)
            query_acc = query_acc + jnp.einsum("ngbk,nkd->nbgd", dscore, key_tile) * score_scale
            key_term = jnp.einsum("ngbk,nbgd->nkd", dscore, head_queries) * score_scale
            key_acc = key_acc.at[slot_blocks].add(key_term)
            value_acc = value_acc.at[slot_blocks].add(value_term)
            return (query_acc, key_acc, value_acc), None

        initial = (jnp.zeros((NQB, BLOCK, head_group, HD), jnp.float32),
                   jnp.zeros((NQB, BLOCK, HD), jnp.float32),
                   jnp.zeros((NQB, BLOCK, HD), jnp.float32))
        finals, unused = lax.scan(per_slot, initial, (block_pairs.T, pair_kinds.T))
        return finals

    query_acc, key_acc, value_acc = lax.map(per_head, (query_all, grad_all, key_all, value_all, log_all, delta_all))
    query_grad = query_acc.transpose(1, 2, 0, 3, 4).reshape(TOKENS, QH, HD).astype(jnp.bfloat16)
    key_grad = key_acc.transpose(1, 2, 0, 3).reshape(TOKENS, KVH, HD).astype(jnp.bfloat16)
    value_grad = value_acc.transpose(1, 2, 0, 3).reshape(TOKENS, KVH, HD).astype(jnp.bfloat16)
    return query_grad, key_grad, value_grad
```

```python
from functools import partial

import jax
import jax.numpy as jnp
from jax import lax
from jax.experimental import pallas as pl
from jax.experimental.pallas import tpu as pltpu
from jax.sharding import PartitionSpec as P

BLOCK = 64
MESH = pl.DeviceIdType.MESH


def kernel(
    n_ctx,
    n_head,
    n_slot,
    pair_tab,
    kind_tab,
    q_hbm,
    g_hbm,
    kv_in,
    log_ref,
    delta_ref,
    dq_out,
    dkv_out,
    q_buf,
    g_buf,
    kv_loc,
    outgoing,
    arrived,
    kcat,
    log_rows,
    delta_rows,
    acc,
    acc_hub,
    far_terms,
    dq_buf,
    part,
    ret,
    fin,
    kv_send,
    kv_recv,
    q_send,
    q_recv,
    g_send,
    g_recv,
    arr_send,
    arr_recv,
    dq_send,
    dq_recv,
    ret_send,
    ret_recv,
    fin_send,
    fin_recv,
):
    rank = lax.axis_index("ctx")
    me = lax.axis_index("head")
    rows = q_hbm.shape[0]
    heads = q_hbm.shape[1] // n_head
    width = q_hbm.shape[2]
    per_src = rows // BLOCK
    blocks = per_src * n_head
    lanes = BLOCK * heads
    keys = n_slot * BLOCK
    scale = width ** (-0.5)

    def peer(d):
        return lax.rem(me // 2 + d // 2, n_head // 2) * 2 + lax.rem(
            lax.rem(me, 2) + lax.rem(d, 2), 2
        )

    barrier = pltpu.get_barrier_semaphore()
    for d in range(1, n_head):
        pl.semaphore_signal(barrier, inc=1, device_id=(rank, peer(d)), device_id_type=MESH)

    def greet(k, c):
        pl.semaphore_signal(
            barrier, inc=1, device_id=(lax.rem(rank + k, n_ctx), me), device_id_type=MESH
        )
        return c

    lax.fori_loop(1, n_ctx, greet, 0)
    pl.semaphore_wait(barrier, n_ctx + n_head - 2)

    def kv_copy(p):
        return pltpu.make_async_remote_copy(
            src_ref=kv_in.at[p],
            dst_ref=kv_loc.at[pl.ds(me * per_src, per_src)],
            send_sem=kv_send.at[p],
            recv_sem=kv_recv.at[me],
            device_id=(rank, p),
            device_id_type=MESH,
        )

    def token_copy(src, dst, send, recv, p, j):
        return pltpu.make_async_remote_copy(
            src_ref=src.at[pl.ds(j * BLOCK, BLOCK), pl.ds(pl.multiple_of(p * heads, heads), heads)],
            dst_ref=dst.at[me, j],
            send_sem=send.at[p, j],
            recv_sem=recv.at[me, j],
            device_id=(rank, p),
            device_id_type=MESH,
        )

    def own_copy(src, dst, recv, j):
        return pltpu.make_async_copy(
            src.at[pl.ds(j * BLOCK, BLOCK), pl.ds(pl.multiple_of(me * heads, heads), heads)],
            dst.at[me, j],
            recv.at[me, j],
        )

    far_first = list(range(2, n_head)) + [1]
    for d in far_first:
        kv_copy(peer(d)).start()
    own_kv = pltpu.make_async_copy(
        kv_in.at[me], kv_loc.at[pl.ds(me * per_src, per_src)], kv_recv.at[me]
    )
    own_kv.start()
    for j in range(per_src):
        own_copy(q_hbm, q_buf, q_recv, j).start()
        own_copy(g_hbm, g_buf, g_recv, j).start()
    for j in range(per_src):
        for d in far_first:
            token_copy(q_hbm, q_buf, q_send, q_recv, peer(d), j).start()
            token_copy(g_hbm, g_buf, g_send, g_recv, peer(d), j).start()

    spread = (
        lax.broadcasted_iota(jnp.int32, (BLOCK, lanes), 1) // heads
        == lax.broadcasted_iota(jnp.int32, (BLOCK, lanes), 0)
    ).astype(jnp.float32)
    own_row = lax.broadcasted_iota(jnp.int32, (heads, lanes), 1) % heads == lax.broadcasted_iota(
        jnp.int32, (heads, lanes), 0
    )
    for stat_ref, stat_rows in ((log_ref, log_rows), (delta_ref, delta_rows)):
        for i in range(blocks):
            wide = jnp.dot(
                stat_ref[:, i * BLOCK : (i + 1) * BLOCK],
                spread,
                precision=lax.Precision.HIGHEST,
                preferred_element_type=jnp.float32,
            )
            stat_rows[i] = jnp.sum(jnp.where(own_row, wide, 0.0), axis=0, keepdims=True)
    acc[...] = jnp.zeros_like(acc)
    acc_hub[...] = jnp.zeros_like(acc_hub)

    own_kv.wait()
    for d in range(1, n_head):
        p = peer(d)
        kv_here = kv_loc.at[pl.ds(p * per_src, per_src)]
        pltpu.make_async_copy(kv_here, kv_here, kv_recv.at[p]).wait()

    first = rank * blocks

    def wanted_by(s):
        best = jnp.where(rank + 1 == s, blocks - 1, 0)
        for i in range(blocks):
            at = s * blocks + i
            for j in range(3, n_slot):
                local = pair_tab[j, at] - first
                named = (kind_tab[j, at] > 0) & (local >= 0) & (local < blocks)
                best = jnp.where(named, jnp.maximum(best, local), best)
        return best

    def arr_copy(s):
        return pltpu.make_async_remote_copy(
            src_ref=outgoing.at[s],
            dst_ref=arrived.at[rank],
            send_sem=arr_send.at[s],
            recv_sem=arr_recv.at[rank],
            device_id=(s, me),
            device_id_type=MESH,
        )

    def send_block(s, c):
        outgoing[s] = kv_loc[wanted_by(s)]
        arr_copy(s).start()
        return c

    lax.fori_loop(rank + 1, n_ctx, send_block, 0)
    arrived[rank] = kv_loc[0]

    def take_block(o, c):
        pltpu.make_async_copy(arrived.at[o], arrived.at[o], arr_recv.at[o]).wait()
        return c

    lax.fori_loop(0, rank, take_block, 0)

    key_row = lax.broadcasted_iota(jnp.int32, (keys, lanes), 0)
    causal = (key_row >= BLOCK) | (
        key_row <= lax.broadcasted_iota(jnp.int32, (keys, lanes), 1) // heads
    )

    def dq_copy(p, j):
        return pltpu.make_async_remote_copy(
            src_ref=dq_buf.at[p, j],
            dst_ref=dq_out.at[
                pl.ds(j * BLOCK, BLOCK), pl.ds(pl.multiple_of(me * heads, heads), heads)
            ],
            send_sem=dq_send.at[p, j],
            recv_sem=dq_recv.at[me, j],
            device_id=(rank, p),
            device_id_type=MESH,
        )

    def own_dq(j):
        return pltpu.make_async_copy(
            dq_buf.at[me, j],
            dq_out.at[pl.ds(j * BLOCK, BLOCK), pl.ds(pl.multiple_of(me * heads, heads), heads)],
            dq_recv.at[me, j],
        )

    def far_owner(i, j):
        at = first + i
        return jnp.where(kind_tab[j, at] > 0, lax.div(pair_tab[j, at], blocks), rank)

    def block_step(t, c):
        d = t // per_src
        j = lax.rem(t, per_src)
        p = peer(d)
        i = p * per_src + j
        pltpu.make_async_copy(q_buf.at[p, j], q_buf.at[p, j], q_recv.at[p, j]).wait()
        pltpu.make_async_copy(g_buf.at[p, j], g_buf.at[p, j], g_recv.at[p, j]).wait()
        kcat[0:BLOCK] = kv_loc[i]
        kcat[BLOCK : 2 * BLOCK] = jnp.where(
            i == 0,
            arrived[jnp.maximum(rank - 1, 0)],
            kv_loc[jnp.maximum(i - 1, 0)],
        )
        kcat[2 * BLOCK : 3 * BLOCK] = arrived[0]
        for slot in range(3, n_slot):
            kcat[slot * BLOCK : (slot + 1) * BLOCK] = arrived[far_owner(i, slot)]
        key_tile = kcat[:, :width]
        value_tile = kcat[:, width:]
        q = q_buf[p, j].astype(jnp.float32).reshape(lanes, width).astype(jnp.bfloat16)
        g = g_buf[p, j].astype(jnp.float32).reshape(lanes, width).astype(jnp.bfloat16)
        nt = (((1,), (1,)), ((), ()))
        scores = lax.dot_general(key_tile, q, nt, preferred_element_type=jnp.float32) * scale
        weights = jnp.exp(scores - log_rows[i])
        slot_mask = jnp.ones((keys, 1), jnp.int32)
        slot_row = lax.broadcasted_iota(jnp.int32, (keys, 1), 0) // BLOCK
        for slot in range(1, n_slot):
            kind = kind_tab[slot, first + i]
            slot_mask = jnp.where(slot_row == slot, kind, slot_mask)
        weights = jnp.where(causal & (slot_mask > 0), weights, 0.0)
        rounded = weights.astype(jnp.bfloat16)
        prob_grad = lax.dot_general(value_tile, g, nt, preferred_element_type=jnp.float32)
        dscore = (weights * (prob_grad - delta_rows[i])).astype(jnp.bfloat16)
        dv = jnp.dot(rounded, g, preferred_element_type=jnp.float32)
        dk = jnp.dot(dscore, q, preferred_element_type=jnp.float32)
        dq = lax.dot_general(
            dscore, key_tile, (((0,), (0,)), ((), ())), preferred_element_type=jnp.float32
        )
        dq_buf[p, j] = (dq * scale).reshape(BLOCK, heads, width).astype(jnp.bfloat16)

        @pl.when(d == 0)
        def _():
            own_dq(j).start()

        @pl.when(d > 0)
        def _():
            dq_copy(p, j).start()

        acc[i + 1, :, :width] += dk[:BLOCK]
        acc[i + 1, :, width:] += dv[:BLOCK]
        acc[i, :, :width] += dk[BLOCK : 2 * BLOCK]
        acc[i, :, width:] += dv[BLOCK : 2 * BLOCK]
        acc_hub[:, :width] += dk[2 * BLOCK : 3 * BLOCK]
        acc_hub[:, width:] += dv[2 * BLOCK : 3 * BLOCK]
        for slot in range(3, n_slot):
            far_terms[i, slot - 3, :, :width] = dk[slot * BLOCK : (slot + 1) * BLOCK]
            far_terms[i, slot - 3, :, width:] = dv[slot * BLOCK : (slot + 1) * BLOCK]
        return c

    lax.fori_loop(0, blocks, block_step, 0)

    def ret_copy(o):
        return pltpu.make_async_remote_copy(
            src_ref=part.at[o],
            dst_ref=ret.at[rank],
            send_sem=ret_send.at[o],
            recv_sem=ret_recv.at[rank],
            device_id=(o, me),
            device_id_type=MESH,
        )

    def send_part(o, c):
        terms = jnp.where(o == 0, acc_hub[...], 0.0) + jnp.where(o == rank - 1, acc[0], 0.0)
        for i in range(blocks):
            for slot in range(3, n_slot):
                terms += jnp.where(far_owner(i, slot) == o, far_terms[i, slot - 3], 0.0)
        part[o] = terms
        ret_copy(o).start()
        return c

    lax.fori_loop(0, rank, send_part, 0)

    acc[1] += jnp.where(rank == 0, acc_hub[...], 0.0)

    def take_part(s, c):
        pltpu.make_async_copy(ret.at[s], ret.at[s], ret_recv.at[s]).wait()
        b = wanted_by(s)
        for i in range(blocks):
            acc[i + 1] += jnp.where(b == i, ret[s], 0.0)
        return c

    lax.fori_loop(rank + 1, n_ctx, take_part, 0)

    for i in range(blocks):
        j = i % per_src
        fin[i // per_src, j, :, :width] = (acc[i + 1, :, :width] * scale).astype(jnp.bfloat16)
        fin[i // per_src, j, :, width:] = acc[i + 1, :, width:].astype(jnp.bfloat16)

    def fin_copy(p):
        return pltpu.make_async_remote_copy(
            src_ref=fin.at[p],
            dst_ref=dkv_out.at[me],
            send_sem=fin_send.at[p],
            recv_sem=fin_recv.at[me],
            device_id=(rank, p),
            device_id_type=MESH,
        )

    for d in far_first:
        fin_copy(peer(d)).start()
    own_fin = pltpu.make_async_copy(fin.at[me], dkv_out.at[me], fin_recv.at[me])
    own_fin.start()

    def sent_block(s, c):
        arr_copy(s).wait_send()
        return c

    lax.fori_loop(rank + 1, n_ctx, sent_block, 0)

    def sent_part(o, c):
        ret_copy(o).wait_send()
        return c

    lax.fori_loop(0, rank, sent_part, 0)
    for d in range(1, n_head):
        p = peer(d)
        kv_copy(p).wait_send()
        for j in range(per_src):
            token_copy(q_hbm, q_buf, q_send, q_recv, p, j).wait_send()
            token_copy(g_hbm, g_buf, g_send, g_recv, p, j).wait_send()
            dq_copy(p, j).wait_send()
            dq_here = dq_out.at[
                pl.ds(j * BLOCK, BLOCK), pl.ds(pl.multiple_of(p * heads, heads), heads)
            ]
            pltpu.make_async_copy(dq_here, dq_here, dq_recv.at[p, j]).wait()
        fin_copy(p).wait_send()
        pltpu.make_async_copy(dkv_out.at[p], dkv_out.at[p], fin_recv.at[p]).wait()
    for j in range(per_src):
        own_dq(j).wait()
    own_fin.wait()


def shards(
    n_ctx,
    n_head,
    queries,
    key_states,
    value_states,
    out_grad,
    log_sums,
    row_deltas,
    block_pairs,
    pair_kinds,
):
    rows, all_heads, width = queries.shape
    heads = all_heads // n_head
    n_slot = block_pairs.shape[1]
    per_src = rows // BLOCK
    blocks = per_src * n_head
    lanes = BLOCK * heads
    bf16, f32 = jnp.bfloat16, jnp.float32
    kv = jnp.concatenate([key_states, value_states], axis=-1).transpose(1, 0, 2)
    kv = kv.reshape(n_head, per_src, BLOCK, 2 * width)
    vmem = pl.BlockSpec(memory_space=pltpu.VMEM)
    anywhere = pl.BlockSpec(memory_space=pl.ANY)
    dma = pltpu.SemaphoreType.DMA
    dq, dkv = pl.pallas_call(
        partial(kernel, n_ctx, n_head, n_slot),
        out_shape=(
            jax.ShapeDtypeStruct(queries.shape, bf16),
            jax.ShapeDtypeStruct(kv.shape, bf16),
        ),
        in_specs=[
            pl.BlockSpec(memory_space=pltpu.SMEM),
            pl.BlockSpec(memory_space=pltpu.SMEM),
            anywhere,
            anywhere,
            vmem,
            vmem,
            vmem,
        ],
        out_specs=(anywhere, vmem),
        scratch_shapes=[
            pltpu.VMEM((n_head, per_src, BLOCK, heads, width), bf16),
            pltpu.VMEM((n_head, per_src, BLOCK, heads, width), bf16),
            pltpu.VMEM((blocks, BLOCK, 2 * width), bf16),
            pltpu.VMEM((n_ctx, BLOCK, 2 * width), bf16),
            pltpu.VMEM((n_ctx, BLOCK, 2 * width), bf16),
            pltpu.VMEM((n_slot * BLOCK, 2 * width), bf16),
            pltpu.VMEM((blocks, 1, lanes), f32),
            pltpu.VMEM((blocks, 1, lanes), f32),
            pltpu.VMEM((blocks + 1, BLOCK, 2 * width), f32),
            pltpu.VMEM((BLOCK, 2 * width), f32),
            pltpu.VMEM((blocks, n_slot - 3, BLOCK, 2 * width), f32),
            pltpu.VMEM((n_head, per_src, BLOCK, heads, width), bf16),
            pltpu.VMEM((n_ctx, BLOCK, 2 * width), f32),
            pltpu.VMEM((n_ctx, BLOCK, 2 * width), f32),
            pltpu.VMEM((n_head, per_src, BLOCK, 2 * width), bf16),
            dma((n_head,)),
            dma((n_head,)),
            dma((n_head, per_src)),
            dma((n_head, per_src)),
            dma((n_head, per_src)),
            dma((n_head, per_src)),
            dma((n_ctx,)),
            dma((n_ctx,)),
            dma((n_head, per_src)),
            dma((n_head, per_src)),
            dma((n_ctx,)),
            dma((n_ctx,)),
            dma((n_head,)),
            dma((n_head,)),
        ],
        compiler_params=pltpu.CompilerParams(
            collective_id=0, has_side_effects=True, vmem_limit_bytes=60 * 1024 * 1024
        ),
    )(block_pairs.T, pair_kinds.T, queries, out_grad, kv, log_sums, row_deltas)
    back = dkv.reshape(n_head, rows, 2 * width).transpose(1, 0, 2)
    return dq, back[:, :, :width], back[:, :, width:]


def solution(mesh):
    tokens = P(("ctx", "head"), None, None)
    stats = P("head", "ctx")
    return jax.shard_map(
        partial(shards, mesh.shape["ctx"], mesh.shape["head"]),
        mesh=mesh,
        in_specs=(tokens, tokens, tokens, tokens, stats, stats, P(), P()),
        out_specs=(tokens, tokens, tokens),
        check_vma=False,
    )
```

```python
from functools import partial

import jax
import jax.numpy as jnp
from jax import lax
from jax.experimental import pallas as pl
from jax.experimental.pallas import tpu as pltpu
from jax.sharding import PartitionSpec as P

BLOCK = 64
MESH = pl.DeviceIdType.MESH


def kernel(
    n_ctx,
    n_head,
    n_slot,
    pair_tab,
    kind_tab,
    q_hbm,
    g_hbm,
    k_ref,
    v_ref,
    log_ref,
    delta_ref,
    dq_out,
    dkv_out,
    kv_in,
    q_buf,
    g_buf,
    kv_loc,
    outgoing,
    arrived,
    kcat,
    log_rows,
    delta_rows,
    acc,
    acc_hub,
    far_terms,
    dq_buf,
    part,
    ret,
    fin,
    kv_send,
    kv_recv,
    q_send,
    q_recv,
    g_send,
    g_recv,
    arr_send,
    arr_recv,
    dq_send,
    dq_recv,
    ret_send,
    ret_recv,
    fin_send,
    fin_recv,
):
    rank = lax.axis_index("ctx")
    me = lax.axis_index("head")
    rows = q_hbm.shape[0]
    heads = q_hbm.shape[1] // n_head
    width = q_hbm.shape[2]
    per_src = rows // BLOCK
    blocks = per_src * n_head
    lanes = BLOCK * heads
    keys = n_slot * BLOCK
    scale = width ** (-0.5)

    def peer(d):
        return lax.rem(me // 2 + d // 2, n_head // 2) * 2 + lax.rem(
            lax.rem(me, 2) + lax.rem(d, 2), 2
        )

    barrier = pltpu.get_barrier_semaphore()
    for d in range(1, n_head):
        pl.semaphore_signal(barrier, inc=1, device_id=(rank, peer(d)), device_id_type=MESH)

    def greet(k, c):
        pl.semaphore_signal(
            barrier, inc=1, device_id=(lax.rem(rank + k, n_ctx), me), device_id_type=MESH
        )
        return c

    lax.fori_loop(1, n_ctx, greet, 0)
    for at, source in ((0, k_ref), (width, v_ref)):
        whole = source[...].astype(jnp.float32)
        for h in range(n_head):
            kv_in[h, :, :, at : at + width] = (
                whole[:, h].astype(jnp.bfloat16).reshape(per_src, BLOCK, width)
            )
    pl.semaphore_wait(barrier, n_ctx + n_head - 2)

    def kv_copy(p):
        return pltpu.make_async_remote_copy(
            src_ref=kv_in.at[p],
            dst_ref=kv_loc.at[pl.ds(me * per_src, per_src)],
            send_sem=kv_send.at[p],
            recv_sem=kv_recv.at[me],
            device_id=(rank, p),
            device_id_type=MESH,
        )

    def token_copy(src, dst, send, recv, p, j):
        return pltpu.make_async_remote_copy(
            src_ref=src.at[pl.ds(j * BLOCK, BLOCK), pl.ds(pl.multiple_of(p * heads, heads), heads)],
            dst_ref=dst.at[me, j],
            send_sem=send.at[p, j],
            recv_sem=recv.at[me, j],
            device_id=(rank, p),
            device_id_type=MESH,
        )

    def own_copy(src, dst, recv, j):
        return pltpu.make_async_copy(
            src.at[pl.ds(j * BLOCK, BLOCK), pl.ds(pl.multiple_of(me * heads, heads), heads)],
            dst.at[me, j],
            recv.at[me, j],
        )

    far_first = list(range(2, n_head)) + [1]
    for d in far_first:
        kv_copy(peer(d)).start()
    own_kv = pltpu.make_async_copy(
        kv_in.at[me], kv_loc.at[pl.ds(me * per_src, per_src)], kv_recv.at[me]
    )
    own_kv.start()
    for j in range(per_src):
        own_copy(q_hbm, q_buf, q_recv, j).start()
        own_copy(g_hbm, g_buf, g_recv, j).start()
    for j in range(per_src):
        for d in far_first:
            token_copy(q_hbm, q_buf, q_send, q_recv, peer(d), j).start()
            token_copy(g_hbm, g_buf, g_send, g_recv, peer(d), j).start()

    spread = (
        lax.broadcasted_iota(jnp.int32, (BLOCK, lanes), 1) // heads
        == lax.broadcasted_iota(jnp.int32, (BLOCK, lanes), 0)
    ).astype(jnp.float32)
    own_row = lax.broadcasted_iota(jnp.int32, (heads, lanes), 1) % heads == lax.broadcasted_iota(
        jnp.int32, (heads, lanes), 0
    )
    for stat_ref, stat_rows in ((log_ref, log_rows), (delta_ref, delta_rows)):
        for i in range(blocks):
            wide = jnp.dot(
                stat_ref[:, i * BLOCK : (i + 1) * BLOCK],
                spread,
                precision=lax.Precision.HIGHEST,
                preferred_element_type=jnp.float32,
            )
            stat_rows[i] = jnp.sum(jnp.where(own_row, wide, 0.0), axis=0, keepdims=True)
    acc[...] = jnp.zeros_like(acc)
    acc_hub[...] = jnp.zeros_like(acc_hub)

    own_kv.wait()
    for d in range(1, n_head):
        p = peer(d)
        kv_here = kv_loc.at[pl.ds(p * per_src, per_src)]
        pltpu.make_async_copy(kv_here, kv_here, kv_recv.at[p]).wait()

    first = rank * blocks

    def wanted_by(s):
        best = jnp.where(rank + 1 == s, blocks - 1, 0)
        for i in range(blocks):
            at = s * blocks + i
            for j in range(3, n_slot):
                local = pair_tab[j, at] - first
                named = (kind_tab[j, at] > 0) & (local >= 0) & (local < blocks)
                best = jnp.where(named, jnp.maximum(best, local), best)
        return best

    def arr_copy(s):
        return pltpu.make_async_remote_copy(
            src_ref=outgoing.at[s],
            dst_ref=arrived.at[rank],
            send_sem=arr_send.at[s],
            recv_sem=arr_recv.at[rank],
            device_id=(s, me),
            device_id_type=MESH,
        )

    def send_block(s, c):
        outgoing[s] = kv_loc[wanted_by(s)]
        arr_copy(s).start()
        return c

    lax.fori_loop(rank + 1, n_ctx, send_block, 0)
    arrived[rank] = kv_loc[0]

    def take_block(o, c):
        pltpu.make_async_copy(arrived.at[o], arrived.at[o], arr_recv.at[o]).wait()
        return c

    lax.fori_loop(0, rank, take_block, 0)

    key_row = lax.broadcasted_iota(jnp.int32, (keys, lanes), 0)
    causal = (key_row >= BLOCK) | (
        key_row <= lax.broadcasted_iota(jnp.int32, (keys, lanes), 1) // heads
    )

    def dq_copy(p, j):
        return pltpu.make_async_remote_copy(
            src_ref=dq_buf.at[p, j],
            dst_ref=dq_out.at[
                pl.ds(j * BLOCK, BLOCK), pl.ds(pl.multiple_of(me * heads, heads), heads)
            ],
            send_sem=dq_send.at[p, j],
            recv_sem=dq_recv.at[me, j],
            device_id=(rank, p),
            device_id_type=MESH,
        )

    def own_dq(j):
        return pltpu.make_async_copy(
            dq_buf.at[me, j],
            dq_out.at[pl.ds(j * BLOCK, BLOCK), pl.ds(pl.multiple_of(me * heads, heads), heads)],
            dq_recv.at[me, j],
        )

    def far_owner(i, j):
        at = first + i
        return jnp.where(kind_tab[j, at] > 0, lax.div(pair_tab[j, at], blocks), rank)

    def block_step(t, c):
        d = t // (2 * per_src) * 2 + lax.rem(t, 2)
        j = lax.rem(t // 2, per_src)
        p = peer(d)
        i = p * per_src + j
        pltpu.make_async_copy(q_buf.at[p, j], q_buf.at[p, j], q_recv.at[p, j]).wait()
        pltpu.make_async_copy(g_buf.at[p, j], g_buf.at[p, j], g_recv.at[p, j]).wait()
        kcat[0:BLOCK] = kv_loc[i]
        kcat[BLOCK : 2 * BLOCK] = jnp.where(
            i == 0,
            arrived[jnp.maximum(rank - 1, 0)],
            kv_loc[jnp.maximum(i - 1, 0)],
        )
        kcat[2 * BLOCK : 3 * BLOCK] = arrived[0]
        for slot in range(3, n_slot):
            kcat[slot * BLOCK : (slot + 1) * BLOCK] = arrived[far_owner(i, slot)]
        key_tile = kcat[:, :width]
        value_tile = kcat[:, width:]
        q = q_buf[p, j].astype(jnp.float32).reshape(lanes, width).astype(jnp.bfloat16)
        g = g_buf[p, j].astype(jnp.float32).reshape(lanes, width).astype(jnp.bfloat16)
        nt = (((1,), (1,)), ((), ()))
        scores = lax.dot_general(key_tile, q, nt, preferred_element_type=jnp.float32) * scale
        weights = jnp.exp(scores - log_rows[i])
        slot_mask = jnp.ones((keys, 1), jnp.int32)
        slot_row = lax.broadcasted_iota(jnp.int32, (keys, 1), 0) // BLOCK
        for slot in range(1, n_slot):
            kind = kind_tab[slot, first + i]
            slot_mask = jnp.where(slot_row == slot, kind, slot_mask)
        weights = jnp.where(causal & (slot_mask > 0), weights, 0.0)
        rounded = weights.astype(jnp.bfloat16)
        prob_grad = lax.dot_general(value_tile, g, nt, preferred_element_type=jnp.float32)
        dscore = (weights * (prob_grad - delta_rows[i])).astype(jnp.bfloat16)
        dv = jnp.dot(rounded, g, preferred_element_type=jnp.float32)
        dk = jnp.dot(dscore, q, preferred_element_type=jnp.float32)
        dq = lax.dot_general(
            dscore, key_tile, (((0,), (0,)), ((), ())), preferred_element_type=jnp.float32
        )
        dq_buf[p, j] = (dq * scale).reshape(BLOCK, heads, width).astype(jnp.bfloat16)

        @pl.when(d == 0)
        def _():
            own_dq(j).start()

        @pl.when(d > 0)
        def _():
            dq_copy(p, j).start()

        for u, terms in enumerate((dk, dv)):
            acc[u, i + 1] += terms[:BLOCK]
            acc[u, i] += terms[BLOCK : 2 * BLOCK]
            acc_hub[u] += terms[2 * BLOCK : 3 * BLOCK]
            for slot in range(3, n_slot):
                far_terms[u, i, slot - 3] = terms[slot * BLOCK : (slot + 1) * BLOCK]
        return c

    lax.fori_loop(0, blocks, block_step, 0)

    def ret_copy(u, o):
        return pltpu.make_async_remote_copy(
            src_ref=part.at[u, o],
            dst_ref=ret.at[u, rank],
            send_sem=ret_send.at[u, o],
            recv_sem=ret_recv.at[u, rank],
            device_id=(o, me),
            device_id_type=MESH,
        )

    def send_part(u, o):
        terms = jnp.where(o == 0, acc_hub[u], 0.0) + jnp.where(o == rank - 1, acc[u, 0], 0.0)
        for i in range(blocks):
            for slot in range(3, n_slot):
                terms += jnp.where(far_owner(i, slot) == o, far_terms[u, i, slot - 3], 0.0)
        part[u, o] = terms
        ret_copy(u, o).start()

    def take_part(u, s):
        pltpu.make_async_copy(ret.at[u, s], ret.at[u, s], ret_recv.at[u, s]).wait()
        b = wanted_by(s)
        for i in range(blocks):
            acc[u, i + 1] += jnp.where(b == i, ret[u, s], 0.0)

    def fin_copy(u, p):
        return pltpu.make_async_remote_copy(
            src_ref=fin.at[u, p],
            dst_ref=dkv_out.at[u, me],
            send_sem=fin_send.at[u, p],
            recv_sem=fin_recv.at[u, me],
            device_id=(rank, p),
            device_id_type=MESH,
        )

    def own_fin(u):
        return pltpu.make_async_copy(fin.at[u, me], dkv_out.at[u, me], fin_recv.at[u, me])

    def each(step, u):
        def body(k, c):
            step(u, k)
            return c

        return body

    for u in range(2):
        lax.fori_loop(0, rank, each(send_part, u), 0)
    for u in range(2):
        acc[u, 1] += jnp.where(rank == 0, acc_hub[u], 0.0)
        lax.fori_loop(rank + 1, n_ctx, each(take_part, u), 0)
        for i in range(blocks):
            fin[u, i // per_src, i % per_src] = (
                acc[u, i + 1] * scale if u == 0 else acc[u, i + 1]
            ).astype(jnp.bfloat16)
        for d in far_first:
            fin_copy(u, peer(d)).start()
        own_fin(u).start()

    def sent_block(s, c):
        arr_copy(s).wait_send()
        return c

    lax.fori_loop(rank + 1, n_ctx, sent_block, 0)

    def sent_part(o, c):
        ret_copy(0, o).wait_send()
        ret_copy(1, o).wait_send()
        return c

    lax.fori_loop(0, rank, sent_part, 0)
    for d in range(1, n_head):
        p = peer(d)
        kv_copy(p).wait_send()
        for j in range(per_src):
            token_copy(q_hbm, q_buf, q_send, q_recv, p, j).wait_send()
            token_copy(g_hbm, g_buf, g_send, g_recv, p, j).wait_send()
            dq_copy(p, j).wait_send()
            dq_here = dq_out.at[
                pl.ds(j * BLOCK, BLOCK), pl.ds(pl.multiple_of(p * heads, heads), heads)
            ]
            pltpu.make_async_copy(dq_here, dq_here, dq_recv.at[p, j]).wait()
        for u in range(2):
            fin_copy(u, p).wait_send()
            fin_here = dkv_out.at[u, p]
            pltpu.make_async_copy(fin_here, fin_here, fin_recv.at[u, p]).wait()
    for j in range(per_src):
        own_dq(j).wait()
    for u in range(2):
        own_fin(u).wait()


def tail(dq_in, dkv_in, dq_out, dk_out, dv_out, staged, sems):
    load = pltpu.make_async_copy(dq_in, staged, sems.at[0])
    load.start()
    n_head, per_src, block, width = dkv_in.shape[1:]
    for u, out in enumerate((dk_out, dv_out)):
        by_head = dkv_in[u].astype(jnp.float32).reshape(n_head, per_src * block, width)
        out[...] = jnp.stack([by_head[h] for h in range(n_head)], axis=1).astype(jnp.bfloat16)
    load.wait()
    store = pltpu.make_async_copy(staged, dq_out, sems.at[1])
    store.start()
    store.wait()


def shards(
    n_ctx,
    n_head,
    queries,
    key_states,
    value_states,
    out_grad,
    log_sums,
    row_deltas,
    block_pairs,
    pair_kinds,
):
    rows, all_heads, width = queries.shape
    heads = all_heads // n_head
    n_slot = block_pairs.shape[1]
    per_src = rows // BLOCK
    blocks = per_src * n_head
    lanes = BLOCK * heads
    bf16, f32 = jnp.bfloat16, jnp.float32
    half = (2, n_head, per_src, BLOCK, width)
    vmem = pl.BlockSpec(memory_space=pltpu.VMEM)
    anywhere = pl.BlockSpec(memory_space=pl.ANY)
    dma = pltpu.SemaphoreType.DMA
    dq, dkv = pl.pallas_call(
        partial(kernel, n_ctx, n_head, n_slot),
        out_shape=(
            jax.ShapeDtypeStruct(queries.shape, bf16),
            jax.ShapeDtypeStruct(half, bf16),
        ),
        in_specs=[
            pl.BlockSpec(memory_space=pltpu.SMEM),
            pl.BlockSpec(memory_space=pltpu.SMEM),
            anywhere,
            anywhere,
            vmem,
            vmem,
            vmem,
            vmem,
        ],
        out_specs=(anywhere, vmem),
        scratch_shapes=[
            pltpu.VMEM((n_head, per_src, BLOCK, 2 * width), bf16),
            pltpu.VMEM((n_head, per_src, BLOCK, heads, width), bf16),
            pltpu.VMEM((n_head, per_src, BLOCK, heads, width), bf16),
            pltpu.VMEM((blocks, BLOCK, 2 * width), bf16),
            pltpu.VMEM((n_ctx, BLOCK, 2 * width), bf16),
            pltpu.VMEM((n_ctx, BLOCK, 2 * width), bf16),
            pltpu.VMEM((n_slot * BLOCK, 2 * width), bf16),
            pltpu.VMEM((blocks, 1, lanes), f32),
            pltpu.VMEM((blocks, 1, lanes), f32),
            pltpu.VMEM((2, blocks + 1, BLOCK, width), f32),
            pltpu.VMEM((2, BLOCK, width), f32),
            pltpu.VMEM((2, blocks, n_slot - 3, BLOCK, width), f32),
            pltpu.VMEM((n_head, per_src, BLOCK, heads, width), bf16),
            pltpu.VMEM((2, n_ctx, BLOCK, width), f32),
            pltpu.VMEM((2, n_ctx, BLOCK, width), f32),
            pltpu.VMEM(half, bf16),
            dma((n_head,)),
            dma((n_head,)),
            dma((n_head, per_src)),
            dma((n_head, per_src)),
            dma((n_head, per_src)),
            dma((n_head, per_src)),
            dma((n_ctx,)),
            dma((n_ctx,)),
            dma((n_head, per_src)),
            dma((n_head, per_src)),
            dma((2, n_ctx)),
            dma((2, n_ctx)),
            dma((2, n_head)),
            dma((2, n_head)),
        ],
        compiler_params=pltpu.CompilerParams(
            collective_id=0, has_side_effects=True, vmem_limit_bytes=60 * 1024 * 1024
        ),
    )(block_pairs.T, pair_kinds.T, queries, out_grad, key_states, value_states, log_sums, row_deltas)
    return pl.pallas_call(
        tail,
        out_shape=(
            jax.ShapeDtypeStruct(queries.shape, bf16),
            jax.ShapeDtypeStruct(key_states.shape, bf16),
            jax.ShapeDtypeStruct(value_states.shape, bf16),
        ),
        in_specs=[anywhere, vmem],
        out_specs=(anywhere, vmem, vmem),
        scratch_shapes=[pltpu.VMEM(queries.shape, bf16), dma((2,))],
    )(dq, dkv)


def solution(mesh):
    tokens = P(("ctx", "head"), None, None)
    stats = P("head", "ctx")
    return jax.shard_map(
        partial(shards, mesh.shape["ctx"], mesh.shape["head"]),
        mesh=mesh,
        in_specs=(tokens, tokens, tokens, tokens, stats, stats, P(), P()),
        out_specs=(tokens, tokens, tokens),
        check_vma=False,
    )
```

```python
from functools import partial

import jax
import jax.numpy as jnp
from jax import lax
from jax.experimental import pallas as pl
from jax.experimental.pallas import tpu as pltpu
from jax.sharding import PartitionSpec as P

BLOCK = 64
MESH = pl.DeviceIdType.MESH


def kernel(
    n_ctx,
    n_head,
    n_slot,
    pair_tab,
    kind_tab,
    q_hbm,
    g_hbm,
    k_ref,
    v_ref,
    log_ref,
    delta_ref,
    dq_out,
    dk_out,
    dv_land,
    kv_in,
    q_buf,
    g_buf,
    kv_loc,
    outgoing,
    arrived,
    kcat,
    log_rows,
    delta_rows,
    acc,
    acc_hub,
    far_terms,
    dq_buf,
    part,
    ret,
    fin,
    dk_land,
    kv_send,
    kv_recv,
    q_send,
    q_recv,
    g_send,
    g_recv,
    arr_send,
    arr_recv,
    dq_send,
    dq_recv,
    ret_send,
    ret_recv,
    fin_send,
    fin_recv,
):
    rank = lax.axis_index("ctx")
    me = lax.axis_index("head")
    rows = q_hbm.shape[0]
    heads = q_hbm.shape[1] // n_head
    width = q_hbm.shape[2]
    per_src = rows // BLOCK
    blocks = per_src * n_head
    lanes = BLOCK * heads
    keys = n_slot * BLOCK
    scale = width ** (-0.5)

    def peer(d):
        return lax.rem(me // 2 + d // 2, n_head // 2) * 2 + lax.rem(
            lax.rem(me, 2) + lax.rem(d, 2), 2
        )

    barrier = pltpu.get_barrier_semaphore()
    for d in range(1, n_head):
        pl.semaphore_signal(barrier, inc=1, device_id=(rank, peer(d)), device_id_type=MESH)

    def greet(k, c):
        pl.semaphore_signal(
            barrier, inc=1, device_id=(lax.rem(rank + k, n_ctx), me), device_id_type=MESH
        )
        return c

    lax.fori_loop(1, n_ctx, greet, 0)
    for at, source in ((0, k_ref), (width, v_ref)):
        whole = source[...].astype(jnp.float32)
        for h in range(n_head):
            kv_in[h, :, :, at : at + width] = (
                whole[:, h].astype(jnp.bfloat16).reshape(per_src, BLOCK, width)
            )
    pl.semaphore_wait(barrier, n_ctx + n_head - 2)

    def kv_copy(p):
        return pltpu.make_async_remote_copy(
            src_ref=kv_in.at[p],
            dst_ref=kv_loc.at[pl.ds(me * per_src, per_src)],
            send_sem=kv_send.at[p],
            recv_sem=kv_recv.at[me],
            device_id=(rank, p),
            device_id_type=MESH,
        )

    def token_copy(src, dst, send, recv, p, j):
        return pltpu.make_async_remote_copy(
            src_ref=src.at[pl.ds(j * BLOCK, BLOCK), pl.ds(pl.multiple_of(p * heads, heads), heads)],
            dst_ref=dst.at[me, j],
            send_sem=send.at[p, j],
            recv_sem=recv.at[me, j],
            device_id=(rank, p),
            device_id_type=MESH,
        )

    def own_copy(src, dst, recv, j):
        return pltpu.make_async_copy(
            src.at[pl.ds(j * BLOCK, BLOCK), pl.ds(pl.multiple_of(me * heads, heads), heads)],
            dst.at[me, j],
            recv.at[me, j],
        )

    far_first = list(range(2, n_head)) + [1]
    for d in far_first:
        kv_copy(peer(d)).start()
    own_kv = pltpu.make_async_copy(
        kv_in.at[me], kv_loc.at[pl.ds(me * per_src, per_src)], kv_recv.at[me]
    )
    own_kv.start()
    for j in range(per_src):
        own_copy(q_hbm, q_buf, q_recv, j).start()
        own_copy(g_hbm, g_buf, g_recv, j).start()
    for j in range(per_src):
        for d in far_first:
            token_copy(q_hbm, q_buf, q_send, q_recv, peer(d), j).start()
            token_copy(g_hbm, g_buf, g_send, g_recv, peer(d), j).start()

    spread = (
        lax.broadcasted_iota(jnp.int32, (BLOCK, lanes), 1) // heads
        == lax.broadcasted_iota(jnp.int32, (BLOCK, lanes), 0)
    ).astype(jnp.float32)
    own_row = lax.broadcasted_iota(jnp.int32, (heads, lanes), 1) % heads == lax.broadcasted_iota(
        jnp.int32, (heads, lanes), 0
    )
    for stat_ref, stat_rows in ((log_ref, log_rows), (delta_ref, delta_rows)):
        for i in range(blocks):
            wide = jnp.dot(
                stat_ref[:, i * BLOCK : (i + 1) * BLOCK],
                spread,
                precision=lax.Precision.HIGHEST,
                preferred_element_type=jnp.float32,
            )
            stat_rows[i] = jnp.sum(jnp.where(own_row, wide, 0.0), axis=0, keepdims=True)
    acc[...] = jnp.zeros_like(acc)
    acc_hub[...] = jnp.zeros_like(acc_hub)

    own_kv.wait()
    for d in range(1, n_head):
        p = peer(d)
        kv_here = kv_loc.at[pl.ds(p * per_src, per_src)]
        pltpu.make_async_copy(kv_here, kv_here, kv_recv.at[p]).wait()

    first = rank * blocks

    def wanted_by(s):
        best = jnp.where(rank + 1 == s, blocks - 1, 0)
        for i in range(blocks):
            at = s * blocks + i
            for j in range(3, n_slot):
                local = pair_tab[j, at] - first
                named = (kind_tab[j, at] > 0) & (local >= 0) & (local < blocks)
                best = jnp.where(named, jnp.maximum(best, local), best)
        return best

    def arr_copy(s):
        return pltpu.make_async_remote_copy(
            src_ref=outgoing.at[s],
            dst_ref=arrived.at[rank],
            send_sem=arr_send.at[s],
            recv_sem=arr_recv.at[rank],
            device_id=(s, me),
            device_id_type=MESH,
        )

    def send_block(s, c):
        outgoing[s] = kv_loc[wanted_by(s)]
        arr_copy(s).start()
        return c

    lax.fori_loop(rank + 1, n_ctx, send_block, 0)
    arrived[rank] = kv_loc[0]

    def take_block(o, c):
        pltpu.make_async_copy(arrived.at[o], arrived.at[o], arr_recv.at[o]).wait()
        return c

    lax.fori_loop(0, rank, take_block, 0)

    key_row = lax.broadcasted_iota(jnp.int32, (keys, lanes), 0)
    causal = (key_row >= BLOCK) | (
        key_row <= lax.broadcasted_iota(jnp.int32, (keys, lanes), 1) // heads
    )

    def dq_copy(p, j):
        return pltpu.make_async_remote_copy(
            src_ref=dq_buf.at[p, j],
            dst_ref=dq_out.at[
                pl.ds(j * BLOCK, BLOCK), pl.ds(pl.multiple_of(me * heads, heads), heads)
            ],
            send_sem=dq_send.at[p, j],
            recv_sem=dq_recv.at[me, j],
            device_id=(rank, p),
            device_id_type=MESH,
        )

    def own_dq(j):
        return pltpu.make_async_copy(
            dq_buf.at[me, j],
            dq_out.at[pl.ds(j * BLOCK, BLOCK), pl.ds(pl.multiple_of(me * heads, heads), heads)],
            dq_recv.at[me, j],
        )

    def far_owner(i, j):
        at = first + i
        return jnp.where(kind_tab[j, at] > 0, lax.div(pair_tab[j, at], blocks), rank)

    def block_step(t, c):
        d = t // (2 * per_src) * 2 + lax.rem(t, 2)
        j = lax.rem(t // 2, per_src)
        p = peer(d)
        i = p * per_src + j
        pltpu.make_async_copy(q_buf.at[p, j], q_buf.at[p, j], q_recv.at[p, j]).wait()
        pltpu.make_async_copy(g_buf.at[p, j], g_buf.at[p, j], g_recv.at[p, j]).wait()
        kcat[0:BLOCK] = kv_loc[i]
        kcat[BLOCK : 2 * BLOCK] = jnp.where(
            i == 0,
            arrived[jnp.maximum(rank - 1, 0)],
            kv_loc[jnp.maximum(i - 1, 0)],
        )
        kcat[2 * BLOCK : 3 * BLOCK] = arrived[0]
        for slot in range(3, n_slot):
            kcat[slot * BLOCK : (slot + 1) * BLOCK] = arrived[far_owner(i, slot)]
        key_tile = kcat[:, :width]
        value_tile = kcat[:, width:]
        q = q_buf[p, j].astype(jnp.float32).reshape(lanes, width).astype(jnp.bfloat16)
        g = g_buf[p, j].astype(jnp.float32).reshape(lanes, width).astype(jnp.bfloat16)
        nt = (((1,), (1,)), ((), ()))
        scores = lax.dot_general(key_tile, q, nt, preferred_element_type=jnp.float32) * scale
        weights = jnp.exp(scores - log_rows[i])
        slot_mask = jnp.ones((keys, 1), jnp.int32)
        slot_row = lax.broadcasted_iota(jnp.int32, (keys, 1), 0) // BLOCK
        for slot in range(1, n_slot):
            kind = kind_tab[slot, first + i]
            slot_mask = jnp.where(slot_row == slot, kind, slot_mask)
        weights = jnp.where(causal & (slot_mask > 0), weights, 0.0)
        rounded = weights.astype(jnp.bfloat16)
        prob_grad = lax.dot_general(value_tile, g, nt, preferred_element_type=jnp.float32)
        dscore = (weights * (prob_grad - delta_rows[i])).astype(jnp.bfloat16)
        dv = jnp.dot(rounded, g, preferred_element_type=jnp.float32)
        dk = jnp.dot(dscore, q, preferred_element_type=jnp.float32)
        dq = lax.dot_general(
            dscore, key_tile, (((0,), (0,)), ((), ())), preferred_element_type=jnp.float32
        )
        dq_buf[p, j] = (dq * scale).reshape(BLOCK, heads, width).astype(jnp.bfloat16)

        @pl.when(d == 0)
        def _():
            own_dq(j).start()

        @pl.when(d > 0)
        def _():
            dq_copy(p, j).start()

        for u, terms in enumerate((dk, dv)):
            acc[u, i + 1] += terms[:BLOCK]
            acc[u, i] += terms[BLOCK : 2 * BLOCK]
            acc_hub[u] += terms[2 * BLOCK : 3 * BLOCK]
            for slot in range(3, n_slot):
                far_terms[u, i, slot - 3] = terms[slot * BLOCK : (slot + 1) * BLOCK]
        return c

    lax.fori_loop(0, blocks, block_step, 0)

    def ret_copy(u, o):
        return pltpu.make_async_remote_copy(
            src_ref=part.at[u, o],
            dst_ref=ret.at[u, rank],
            send_sem=ret_send.at[u, o],
            recv_sem=ret_recv.at[u, rank],
            device_id=(o, me),
            device_id_type=MESH,
        )

    def send_part(u, o):
        terms = jnp.where(o == 0, acc_hub[u], 0.0) + jnp.where(o == rank - 1, acc[u, 0], 0.0)
        for i in range(blocks):
            for slot in range(3, n_slot):
                terms += jnp.where(far_owner(i, slot) == o, far_terms[u, i, slot - 3], 0.0)
        part[u, o] = terms
        ret_copy(u, o).start()

    def take_part(u, s):
        pltpu.make_async_copy(ret.at[u, s], ret.at[u, s], ret_recv.at[u, s]).wait()
        b = wanted_by(s)
        for i in range(blocks):
            acc[u, i + 1] += jnp.where(b == i, ret[u, s], 0.0)

    def fin_copy(u, p):
        return pltpu.make_async_remote_copy(
            src_ref=fin.at[u, p],
            dst_ref=(dk_land, dv_land)[u].at[me],
            send_sem=fin_send.at[u, p],
            recv_sem=fin_recv.at[u, me],
            device_id=(rank, p),
            device_id_type=MESH,
        )

    def own_fin(u):
        return pltpu.make_async_copy(
            fin.at[u, me], (dk_land, dv_land)[u].at[me], fin_recv.at[u, me]
        )

    def each(step, u):
        def body(k, c):
            step(u, k)
            return c

        return body

    for u in range(2):
        lax.fori_loop(0, rank, each(send_part, u), 0)
    for u in range(2):
        acc[u, 1] += jnp.where(rank == 0, acc_hub[u], 0.0)
        lax.fori_loop(rank + 1, n_ctx, each(take_part, u), 0)
        for i in range(blocks):
            fin[u, i // per_src, i % per_src] = (
                acc[u, i + 1] * scale if u == 0 else acc[u, i + 1]
            ).astype(jnp.bfloat16)
        for d in far_first:
            fin_copy(u, peer(d)).start()
        own_fin(u).start()

    def take_fin(u, land):
        own_fin(u).wait()
        for d in range(1, n_head):
            p = peer(d)
            pltpu.make_async_copy(land.at[p], land.at[p], fin_recv.at[u, p]).wait()

    take_fin(0, dk_land)
    dk_out[...] = by_token(dk_land)

    def sent_block(s, c):
        arr_copy(s).wait_send()
        return c

    lax.fori_loop(rank + 1, n_ctx, sent_block, 0)

    def sent_part(o, c):
        ret_copy(0, o).wait_send()
        ret_copy(1, o).wait_send()
        return c

    lax.fori_loop(0, rank, sent_part, 0)
    for d in range(1, n_head):
        p = peer(d)
        kv_copy(p).wait_send()
        for j in range(per_src):
            token_copy(q_hbm, q_buf, q_send, q_recv, p, j).wait_send()
            token_copy(g_hbm, g_buf, g_send, g_recv, p, j).wait_send()
            dq_copy(p, j).wait_send()
            dq_here = dq_out.at[
                pl.ds(j * BLOCK, BLOCK), pl.ds(pl.multiple_of(p * heads, heads), heads)
            ]
            pltpu.make_async_copy(dq_here, dq_here, dq_recv.at[p, j]).wait()
        for u in range(2):
            fin_copy(u, p).wait_send()
    for j in range(per_src):
        own_dq(j).wait()
    take_fin(1, dv_land)


def by_token(land):
    n_head, per_src, block, width = land.shape
    heads = land[...].astype(jnp.float32).reshape(n_head, per_src * block, width)
    return jnp.stack([heads[h] for h in range(n_head)], axis=1).astype(land.dtype)


def tail(dq_in, dk_in, dv_in, dq_out, dk_out, dv_out, dq_held, dk_held, loads, stores):
    pieces = loads.shape[0] - 1
    step = dq_held.shape[0] // pieces
    parts = [pl.ds(k * step, step) for k in range(pieces)]
    routes = [(dq_in.at[at], dq_held.at[at], dq_out.at[at]) for at in parts]
    routes.append((dk_in, dk_held, dk_out))
    for k, (source, held, _) in enumerate(routes):
        pltpu.make_async_copy(source, held, loads.at[k]).start()
    for k, (source, held, target) in enumerate(routes):
        pltpu.make_async_copy(source, held, loads.at[k]).wait()
        pltpu.make_async_copy(held, target, stores.at[k]).start()
    dv_out[...] = by_token(dv_in)
    for k, (_, held, target) in enumerate(routes):
        pltpu.make_async_copy(held, target, stores.at[k]).wait()


def shards(
    n_ctx,
    n_head,
    queries,
    key_states,
    value_states,
    out_grad,
    log_sums,
    row_deltas,
    block_pairs,
    pair_kinds,
):
    rows, all_heads, width = queries.shape
    heads = all_heads // n_head
    n_slot = block_pairs.shape[1]
    per_src = rows // BLOCK
    blocks = per_src * n_head
    lanes = BLOCK * heads
    bf16, f32 = jnp.bfloat16, jnp.float32
    half = (n_head, per_src, BLOCK, width)
    vmem = pl.BlockSpec(memory_space=pltpu.VMEM)
    anywhere = pl.BlockSpec(memory_space=pl.ANY)
    dma = pltpu.SemaphoreType.DMA
    dq, dk, dv = pl.pallas_call(
        partial(kernel, n_ctx, n_head, n_slot),
        out_shape=(
            jax.ShapeDtypeStruct(queries.shape, bf16),
            jax.ShapeDtypeStruct(key_states.shape, bf16),
            jax.ShapeDtypeStruct(half, bf16),
        ),
        in_specs=[
            pl.BlockSpec(memory_space=pltpu.SMEM),
            pl.BlockSpec(memory_space=pltpu.SMEM),
            anywhere,
            anywhere,
            vmem,
            vmem,
            vmem,
            vmem,
        ],
        out_specs=(anywhere, vmem, vmem),
        scratch_shapes=[
            pltpu.VMEM((n_head, per_src, BLOCK, 2 * width), bf16),
            pltpu.VMEM((n_head, per_src, BLOCK, heads, width), bf16),
            pltpu.VMEM((n_head, per_src, BLOCK, heads, width), bf16),
            pltpu.VMEM((blocks, BLOCK, 2 * width), bf16),
            pltpu.VMEM((n_ctx, BLOCK, 2 * width), bf16),
            pltpu.VMEM((n_ctx, BLOCK, 2 * width), bf16),
            pltpu.VMEM((n_slot * BLOCK, 2 * width), bf16),
            pltpu.VMEM((blocks, 1, lanes), f32),
            pltpu.VMEM((blocks, 1, lanes), f32),
            pltpu.VMEM((2, blocks + 1, BLOCK, width), f32),
            pltpu.VMEM((2, BLOCK, width), f32),
            pltpu.VMEM((2, blocks, n_slot - 3, BLOCK, width), f32),
            pltpu.VMEM((n_head, per_src, BLOCK, heads, width), bf16),
            pltpu.VMEM((2, n_ctx, BLOCK, width), f32),
            pltpu.VMEM((2, n_ctx, BLOCK, width), f32),
            pltpu.VMEM((2,) + half, bf16),
            pltpu.VMEM(half, bf16),
            dma((n_head,)),
            dma((n_head,)),
            dma((n_head, per_src)),
            dma((n_head, per_src)),
            dma((n_head, per_src)),
            dma((n_head, per_src)),
            dma((n_ctx,)),
            dma((n_ctx,)),
            dma((n_head, per_src)),
            dma((n_head, per_src)),
            dma((2, n_ctx)),
            dma((2, n_ctx)),
            dma((2, n_head)),
            dma((2, n_head)),
        ],
        compiler_params=pltpu.CompilerParams(
            collective_id=0, has_side_effects=True, vmem_limit_bytes=60 * 1024 * 1024
        ),
    )(block_pairs.T, pair_kinds.T, queries, out_grad, key_states, value_states, log_sums, row_deltas)
    return pl.pallas_call(
        tail,
        out_shape=(
            jax.ShapeDtypeStruct(queries.shape, bf16),
            jax.ShapeDtypeStruct(key_states.shape, bf16),
            jax.ShapeDtypeStruct(value_states.shape, bf16),
        ),
        in_specs=[anywhere, anywhere, vmem],
        out_specs=(anywhere, anywhere, vmem),
        scratch_shapes=[
            pltpu.VMEM(queries.shape, bf16),
            pltpu.VMEM(key_states.shape, bf16),
            dma((5,)),
            dma((5,)),
        ],
    )(dq, dk, dv)


def solution(mesh):
    tokens = P(("ctx", "head"), None, None)
    stats = P("head", "ctx")
    return jax.shard_map(
        partial(shards, mesh.shape["ctx"], mesh.shape["head"]),
        mesh=mesh,
        in_specs=(tokens, tokens, tokens, tokens, stats, stats, P(), P()),
        out_specs=(tokens, tokens, tokens),
        check_vma=False,
    )
```

```python
from functools import partial

import jax
import jax.numpy as jnp
from jax import lax
from jax.experimental import pallas as pl
from jax.experimental.pallas import tpu as pltpu
from jax.sharding import PartitionSpec as P

BLOCK = 64
MESH = pl.DeviceIdType.MESH


def kernel(
    n_ctx,
    n_head,
    n_slot,
    pair_tab,
    kind_tab,
    q_hbm,
    g_hbm,
    k_ref,
    v_ref,
    log_ref,
    delta_ref,
    dq_out,
    dk_out,
    dv_land,
    wide,
    kv_in,
    q_buf,
    g_buf,
    kv_loc,
    outgoing,
    arrived,
    kcat,
    log_rows,
    delta_rows,
    acc,
    acc_hub,
    far_terms,
    dq_buf,
    part,
    ret,
    fin,
    dk_land,
    kv_send,
    kv_recv,
    q_send,
    q_recv,
    g_send,
    g_recv,
    arr_send,
    arr_recv,
    dq_send,
    dq_recv,
    ret_send,
    ret_recv,
    fin_send,
    fin_recv,
):
    rank = lax.axis_index("ctx")
    me = lax.axis_index("head")
    rows = q_hbm.shape[0]
    heads = q_hbm.shape[1] // n_head
    width = q_hbm.shape[2]
    per_src = rows // BLOCK
    blocks = per_src * n_head
    lanes = BLOCK * heads
    keys = n_slot * BLOCK
    scale = width ** (-0.5)

    def peer(d):
        return lax.rem(me // 2 + d // 2, n_head // 2) * 2 + lax.rem(
            lax.rem(me, 2) + lax.rem(d, 2), 2
        )

    barrier = pltpu.get_barrier_semaphore()
    for d in range(1, n_head):
        pl.semaphore_signal(barrier, inc=1, device_id=(rank, peer(d)), device_id_type=MESH)

    def greet(k, c):
        pl.semaphore_signal(
            barrier, inc=1, device_id=(lax.rem(rank + k, n_ctx), me), device_id_type=MESH
        )
        return c

    lax.fori_loop(1, n_ctx, greet, 0)
    for at, source in ((0, k_ref), (width, v_ref)):
        wide[...] = source[...].astype(jnp.float32)
        for h in range(n_head):
            head_rows = wide[pl.ds(h, rows, stride=n_head), :]
            kv_in[h, :, :, at : at + width] = head_rows.reshape(per_src, BLOCK, width).astype(
                jnp.bfloat16
            )
    pl.semaphore_wait(barrier, n_ctx + n_head - 2)

    def kv_copy(p):
        return pltpu.make_async_remote_copy(
            src_ref=kv_in.at[p],
            dst_ref=kv_loc.at[pl.ds(me * per_src, per_src)],
            send_sem=kv_send.at[p],
            recv_sem=kv_recv.at[me],
            device_id=(rank, p),
            device_id_type=MESH,
        )

    def token_copy(src, dst, send, recv, p, j):
        return pltpu.make_async_remote_copy(
            src_ref=src.at[pl.ds(j * BLOCK, BLOCK), pl.ds(pl.multiple_of(p * heads, heads), heads)],
            dst_ref=dst.at[me, j],
            send_sem=send.at[p, j],
            recv_sem=recv.at[me, j],
            device_id=(rank, p),
            device_id_type=MESH,
        )

    def own_copy(src, dst, recv, j):
        return pltpu.make_async_copy(
            src.at[pl.ds(j * BLOCK, BLOCK), pl.ds(pl.multiple_of(me * heads, heads), heads)],
            dst.at[me, j],
            recv.at[me, j],
        )

    far_first = list(range(2, n_head)) + [1]
    for d in far_first:
        kv_copy(peer(d)).start()
    own_kv = pltpu.make_async_copy(
        kv_in.at[me], kv_loc.at[pl.ds(me * per_src, per_src)], kv_recv.at[me]
    )
    own_kv.start()
    for j in range(per_src):
        own_copy(q_hbm, q_buf, q_recv, j).start()
        own_copy(g_hbm, g_buf, g_recv, j).start()
    for j in range(per_src):
        for d in far_first:
            token_copy(q_hbm, q_buf, q_send, q_recv, peer(d), j).start()
            token_copy(g_hbm, g_buf, g_send, g_recv, peer(d), j).start()

    spread = (
        lax.broadcasted_iota(jnp.int32, (BLOCK, lanes), 1) // heads
        == lax.broadcasted_iota(jnp.int32, (BLOCK, lanes), 0)
    ).astype(jnp.float32)
    own_row = lax.broadcasted_iota(jnp.int32, (heads, lanes), 1) % heads == lax.broadcasted_iota(
        jnp.int32, (heads, lanes), 0
    )
    for stat_ref, stat_rows in ((log_ref, log_rows), (delta_ref, delta_rows)):
        for i in range(blocks):
            by_lane = jnp.dot(
                stat_ref[:, i * BLOCK : (i + 1) * BLOCK],
                spread,
                precision=lax.Precision.HIGHEST,
                preferred_element_type=jnp.float32,
            )
            stat_rows[i] = jnp.sum(jnp.where(own_row, by_lane, 0.0), axis=0, keepdims=True)
    acc[...] = jnp.zeros_like(acc)
    acc_hub[...] = jnp.zeros_like(acc_hub)

    own_kv.wait()
    for d in range(1, n_head):
        p = peer(d)
        kv_here = kv_loc.at[pl.ds(p * per_src, per_src)]
        pltpu.make_async_copy(kv_here, kv_here, kv_recv.at[p]).wait()

    first = rank * blocks

    def wanted_by(s):
        best = jnp.where(rank + 1 == s, blocks - 1, 0)
        for i in range(blocks):
            at = s * blocks + i
            for j in range(3, n_slot):
                local = pair_tab[j, at] - first
                named = (kind_tab[j, at] > 0) & (local >= 0) & (local < blocks)
                best = jnp.where(named, jnp.maximum(best, local), best)
        return best

    def arr_copy(s):
        return pltpu.make_async_remote_copy(
            src_ref=outgoing.at[s],
            dst_ref=arrived.at[rank],
            send_sem=arr_send.at[s],
            recv_sem=arr_recv.at[rank],
            device_id=(s, me),
            device_id_type=MESH,
        )

    def send_block(s, c):
        outgoing[s] = kv_loc[wanted_by(s)]
        arr_copy(s).start()
        return c

    lax.fori_loop(rank + 1, n_ctx, send_block, 0)
    arrived[rank] = kv_loc[0]

    def take_block(o, c):
        pltpu.make_async_copy(arrived.at[o], arrived.at[o], arr_recv.at[o]).wait()
        return c

    lax.fori_loop(0, rank, take_block, 0)

    key_row = lax.broadcasted_iota(jnp.int32, (keys, lanes), 0)
    causal = (key_row >= BLOCK) | (
        key_row <= lax.broadcasted_iota(jnp.int32, (keys, lanes), 1) // heads
    )

    def dq_copy(p, j):
        return pltpu.make_async_remote_copy(
            src_ref=dq_buf.at[p, j],
            dst_ref=dq_out.at[
                pl.ds(j * BLOCK, BLOCK), pl.ds(pl.multiple_of(me * heads, heads), heads)
            ],
            send_sem=dq_send.at[p, j],
            recv_sem=dq_recv.at[me, j],
            device_id=(rank, p),
            device_id_type=MESH,
        )

    def own_dq(j):
        return pltpu.make_async_copy(
            dq_buf.at[me, j],
            dq_out.at[pl.ds(j * BLOCK, BLOCK), pl.ds(pl.multiple_of(me * heads, heads), heads)],
            dq_recv.at[me, j],
        )

    def far_owner(i, j):
        at = first + i
        return jnp.where(kind_tab[j, at] > 0, lax.div(pair_tab[j, at], blocks), rank)

    def block_step(t, c):
        d = t // (2 * per_src) * 2 + lax.rem(t, 2)
        j = lax.rem(t // 2, per_src)
        p = peer(d)
        i = p * per_src + j
        pltpu.make_async_copy(q_buf.at[p, j], q_buf.at[p, j], q_recv.at[p, j]).wait()
        pltpu.make_async_copy(g_buf.at[p, j], g_buf.at[p, j], g_recv.at[p, j]).wait()
        kcat[0:BLOCK] = kv_loc[i]
        kcat[BLOCK : 2 * BLOCK] = jnp.where(
            i == 0,
            arrived[jnp.maximum(rank - 1, 0)],
            kv_loc[jnp.maximum(i - 1, 0)],
        )
        kcat[2 * BLOCK : 3 * BLOCK] = arrived[0]
        for slot in range(3, n_slot):
            kcat[slot * BLOCK : (slot + 1) * BLOCK] = arrived[far_owner(i, slot)]
        key_tile = kcat[:, :width]
        value_tile = kcat[:, width:]
        q = q_buf[p, j].astype(jnp.float32).reshape(lanes, width).astype(jnp.bfloat16)
        g = g_buf[p, j].astype(jnp.float32).reshape(lanes, width).astype(jnp.bfloat16)
        nt = (((1,), (1,)), ((), ()))
        scores = lax.dot_general(key_tile, q, nt, preferred_element_type=jnp.float32) * scale
        weights = jnp.exp(scores - log_rows[i])
        slot_mask = jnp.ones((keys, 1), jnp.int32)
        slot_row = lax.broadcasted_iota(jnp.int32, (keys, 1), 0) // BLOCK
        for slot in range(1, n_slot):
            kind = kind_tab[slot, first + i]
            slot_mask = jnp.where(slot_row == slot, kind, slot_mask)
        weights = jnp.where(causal & (slot_mask > 0), weights, 0.0)
        rounded = weights.astype(jnp.bfloat16)
        prob_grad = lax.dot_general(value_tile, g, nt, preferred_element_type=jnp.float32)
        dscore = (weights * (prob_grad - delta_rows[i])).astype(jnp.bfloat16)
        dv = jnp.dot(rounded, g, preferred_element_type=jnp.float32)
        dk = jnp.dot(dscore, q, preferred_element_type=jnp.float32)
        dq = lax.dot_general(
            dscore, key_tile, (((0,), (0,)), ((), ())), preferred_element_type=jnp.float32
        )
        dq_buf[p, j] = (dq * scale).reshape(BLOCK, heads, width).astype(jnp.bfloat16)

        @pl.when(d == 0)
        def _():
            own_dq(j).start()

        @pl.when(d > 0)
        def _():
            dq_copy(p, j).start()

        for u, terms in enumerate((dk, dv)):
            acc[u, i + 1] += terms[:BLOCK]
            acc[u, i] += terms[BLOCK : 2 * BLOCK]
            acc_hub[u] += terms[2 * BLOCK : 3 * BLOCK]
            for slot in range(3, n_slot):
                far_terms[u, i, slot - 3] = terms[slot * BLOCK : (slot + 1) * BLOCK]
        return c

    lax.fori_loop(0, blocks, block_step, 0)

    def ret_copy(u, o):
        return pltpu.make_async_remote_copy(
            src_ref=part.at[u, o],
            dst_ref=ret.at[u, rank],
            send_sem=ret_send.at[u, o],
            recv_sem=ret_recv.at[u, rank],
            device_id=(o, me),
            device_id_type=MESH,
        )

    def send_part(u, o):
        terms = jnp.where(o == 0, acc_hub[u], 0.0) + jnp.where(o == rank - 1, acc[u, 0], 0.0)
        for i in range(blocks):
            for slot in range(3, n_slot):
                terms += jnp.where(far_owner(i, slot) == o, far_terms[u, i, slot - 3], 0.0)
        part[u, o] = terms
        ret_copy(u, o).start()

    def take_part(u, s):
        pltpu.make_async_copy(ret.at[u, s], ret.at[u, s], ret_recv.at[u, s]).wait()
        b = wanted_by(s)
        for i in range(blocks):
            acc[u, i + 1] += jnp.where(b == i, ret[u, s], 0.0)

    def fin_copy(u, p):
        return pltpu.make_async_remote_copy(
            src_ref=fin.at[u, p],
            dst_ref=(dk_land, dv_land)[u].at[me],
            send_sem=fin_send.at[u, p],
            recv_sem=fin_recv.at[u, me],
            device_id=(rank, p),
            device_id_type=MESH,
        )

    def own_fin(u):
        return pltpu.make_async_copy(
            fin.at[u, me], (dk_land, dv_land)[u].at[me], fin_recv.at[u, me]
        )

    def each(step, u):
        def body(k, c):
            step(u, k)
            return c

        return body

    for u in range(2):
        lax.fori_loop(0, rank, each(send_part, u), 0)
    for u in range(2):
        acc[u, 1] += jnp.where(rank == 0, acc_hub[u], 0.0)
        lax.fori_loop(rank + 1, n_ctx, each(take_part, u), 0)
        for i in range(blocks):
            fin[u, i // per_src, i % per_src] = (
                acc[u, i + 1] * scale if u == 0 else acc[u, i + 1]
            ).astype(jnp.bfloat16)
        for d in far_first:
            fin_copy(u, peer(d)).start()
        own_fin(u).start()

    def take_fin(u, land):
        own_fin(u).wait()
        for d in range(1, n_head):
            p = peer(d)
            pltpu.make_async_copy(land.at[p], land.at[p], fin_recv.at[u, p]).wait()

    take_fin(0, dk_land)
    dk_out[...] = by_token(dk_land, wide)

    def sent_block(s, c):
        arr_copy(s).wait_send()
        return c

    lax.fori_loop(rank + 1, n_ctx, sent_block, 0)

    def sent_part(o, c):
        ret_copy(0, o).wait_send()
        ret_copy(1, o).wait_send()
        return c

    lax.fori_loop(0, rank, sent_part, 0)
    for d in range(1, n_head):
        p = peer(d)
        kv_copy(p).wait_send()
        for j in range(per_src):
            token_copy(q_hbm, q_buf, q_send, q_recv, p, j).wait_send()
            token_copy(g_hbm, g_buf, g_send, g_recv, p, j).wait_send()
            dq_copy(p, j).wait_send()
            dq_here = dq_out.at[
                pl.ds(j * BLOCK, BLOCK), pl.ds(pl.multiple_of(p * heads, heads), heads)
            ]
            pltpu.make_async_copy(dq_here, dq_here, dq_recv.at[p, j]).wait()
        for u in range(2):
            fin_copy(u, p).wait_send()
    for j in range(per_src):
        own_dq(j).wait()
    take_fin(1, dv_land)


def by_token(land, wide):
    n_head, per_src, block, width = land.shape
    rows = per_src * block
    for h in range(n_head):
        wide[pl.ds(h, rows, stride=n_head), :] = (
            land[h].astype(jnp.float32).reshape(rows, width)
        )
    return wide[...].astype(land.dtype)


def tail(dq_in, dk_in, dv_in, dq_out, dk_out, dv_out, dq_held, dk_held, wide, loads, stores):
    pieces = loads.shape[0] - 1
    step = dq_held.shape[0] // pieces
    parts = [pl.ds(k * step, step) for k in range(pieces)]
    routes = [(dq_in.at[at], dq_held.at[at], dq_out.at[at]) for at in parts]
    routes.append((dk_in, dk_held, dk_out))
    for k, (source, held, _) in enumerate(routes):
        pltpu.make_async_copy(source, held, loads.at[k]).start()
    for k, (source, held, target) in enumerate(routes):
        pltpu.make_async_copy(source, held, loads.at[k]).wait()
        pltpu.make_async_copy(held, target, stores.at[k]).start()
    dv_out[...] = by_token(dv_in, wide)
    for k, (_, held, target) in enumerate(routes):
        pltpu.make_async_copy(held, target, stores.at[k]).wait()


def shards(
    n_ctx,
    n_head,
    queries,
    key_states,
    value_states,
    out_grad,
    log_sums,
    row_deltas,
    block_pairs,
    pair_kinds,
):
    rows, all_heads, width = queries.shape
    heads = all_heads // n_head
    n_slot = block_pairs.shape[1]
    per_src = rows // BLOCK
    blocks = per_src * n_head
    lanes = BLOCK * heads
    bf16, f32 = jnp.bfloat16, jnp.float32
    half = (n_head, per_src, BLOCK, width)
    flat = (rows * n_head, width)
    vmem = pl.BlockSpec(memory_space=pltpu.VMEM)
    anywhere = pl.BlockSpec(memory_space=pl.ANY)
    dma = pltpu.SemaphoreType.DMA
    dq, dk, dv = pl.pallas_call(
        partial(kernel, n_ctx, n_head, n_slot),
        out_shape=(
            jax.ShapeDtypeStruct(queries.shape, bf16),
            jax.ShapeDtypeStruct(flat, bf16),
            jax.ShapeDtypeStruct(half, bf16),
        ),
        in_specs=[
            pl.BlockSpec(memory_space=pltpu.SMEM),
            pl.BlockSpec(memory_space=pltpu.SMEM),
            anywhere,
            anywhere,
            vmem,
            vmem,
            vmem,
            vmem,
        ],
        out_specs=(anywhere, vmem, vmem),
        scratch_shapes=[
            pltpu.VMEM(flat, f32),
            pltpu.VMEM((n_head, per_src, BLOCK, 2 * width), bf16),
            pltpu.VMEM((n_head, per_src, BLOCK, heads, width), bf16),
            pltpu.VMEM((n_head, per_src, BLOCK, heads, width), bf16),
            pltpu.VMEM((blocks, BLOCK, 2 * width), bf16),
            pltpu.VMEM((n_ctx, BLOCK, 2 * width), bf16),
            pltpu.VMEM((n_ctx, BLOCK, 2 * width), bf16),
            pltpu.VMEM((n_slot * BLOCK, 2 * width), bf16),
            pltpu.VMEM((blocks, 1, lanes), f32),
            pltpu.VMEM((blocks, 1, lanes), f32),
            pltpu.VMEM((2, blocks + 1, BLOCK, width), f32),
            pltpu.VMEM((2, BLOCK, width), f32),
            pltpu.VMEM((2, blocks, n_slot - 3, BLOCK, width), f32),
            pltpu.VMEM((n_head, per_src, BLOCK, heads, width), bf16),
            pltpu.VMEM((2, n_ctx, BLOCK, width), f32),
            pltpu.VMEM((2, n_ctx, BLOCK, width), f32),
            pltpu.VMEM((2,) + half, bf16),
            pltpu.VMEM(half, bf16),
            dma((n_head,)),
            dma((n_head,)),
            dma((n_head, per_src)),
            dma((n_head, per_src)),
            dma((n_head, per_src)),
            dma((n_head, per_src)),
            dma((n_ctx,)),
            dma((n_ctx,)),
            dma((n_head, per_src)),
            dma((n_head, per_src)),
            dma((2, n_ctx)),
            dma((2, n_ctx)),
            dma((2, n_head)),
            dma((2, n_head)),
        ],
        compiler_params=pltpu.CompilerParams(
            collective_id=0, has_side_effects=True, vmem_limit_bytes=60 * 1024 * 1024
        ),
    )(
        block_pairs.T,
        pair_kinds.T,
        queries,
        out_grad,
        key_states.reshape(flat),
        value_states.reshape(flat),
        log_sums,
        row_deltas,
    )
    dq, dk, dv = pl.pallas_call(
        tail,
        out_shape=(
            jax.ShapeDtypeStruct(queries.shape, bf16),
            jax.ShapeDtypeStruct(flat, bf16),
            jax.ShapeDtypeStruct(flat, bf16),
        ),
        in_specs=[anywhere, anywhere, vmem],
        out_specs=(anywhere, anywhere, vmem),
        scratch_shapes=[
            pltpu.VMEM(queries.shape, bf16),
            pltpu.VMEM(flat, bf16),
            pltpu.VMEM(flat, f32),
            dma((5,)),
            dma((5,)),
        ],
    )(dq, dk, dv)
    return dq, dk.reshape(key_states.shape), dv.reshape(value_states.shape)


def solution(mesh):
    tokens = P(("ctx", "head"), None, None)
    stats = P("head", "ctx")
    return jax.shard_map(
        partial(shards, mesh.shape["ctx"], mesh.shape["head"]),
        mesh=mesh,
        in_specs=(tokens, tokens, tokens, tokens, stats, stats, P(), P()),
        out_specs=(tokens, tokens, tokens),
        check_vma=False,
    )
```

```python
from functools import partial

import jax
import jax.numpy as jnp
from jax import lax
from jax.experimental import pallas as pl
from jax.experimental.pallas import tpu as pltpu
from jax.sharding import PartitionSpec as P

BLOCK = 64
MESH = pl.DeviceIdType.MESH


def kernel(
    n_ctx,
    n_head,
    n_slot,
    pair_tab,
    kind_tab,
    q_hbm,
    g_hbm,
    k_ref,
    v_ref,
    log_ref,
    delta_ref,
    dq_out,
    dk_out,
    dv_land,
    wide,
    kv_in,
    q_buf,
    g_buf,
    kv_loc,
    outgoing,
    arrived,
    kcat,
    log_rows,
    delta_rows,
    acc,
    acc_hub,
    far_terms,
    dq_buf,
    part,
    ret,
    fin,
    dk_land,
    kv_send,
    kv_recv,
    q_send,
    q_recv,
    g_send,
    g_recv,
    arr_send,
    arr_recv,
    dq_send,
    dq_recv,
    ret_send,
    ret_recv,
    fin_send,
    fin_recv,
):
    rank = lax.axis_index("ctx")
    me = lax.axis_index("head")
    rows = q_hbm.shape[0]
    heads = q_hbm.shape[1] // n_head
    width = q_hbm.shape[2]
    per_src = rows // BLOCK
    blocks = per_src * n_head
    lanes = BLOCK * heads
    keys = n_slot * BLOCK
    scale = width ** (-0.5)

    def peer(d):
        return lax.rem(me // 2 + d // 2, n_head // 2) * 2 + lax.rem(
            lax.rem(me, 2) + lax.rem(d, 2), 2
        )

    barrier = pltpu.get_barrier_semaphore()
    for d in range(1, n_head):
        pl.semaphore_signal(barrier, inc=1, device_id=(rank, peer(d)), device_id_type=MESH)

    def greet(k, c):
        pl.semaphore_signal(
            barrier, inc=1, device_id=(lax.rem(rank + k, n_ctx), me), device_id_type=MESH
        )
        return c

    lax.fori_loop(1, n_ctx, greet, 0)
    for at, source in ((0, k_ref), (width, v_ref)):
        wide[...] = source[...].astype(jnp.float32)
        for h in range(n_head):
            head_rows = wide[pl.ds(h, rows, stride=n_head), :]
            kv_in[h, :, :, at : at + width] = head_rows.reshape(per_src, BLOCK, width).astype(
                jnp.bfloat16
            )
    pl.semaphore_wait(barrier, n_ctx + n_head - 2)

    def kv_copy(p):
        return pltpu.make_async_remote_copy(
            src_ref=kv_in.at[p],
            dst_ref=kv_loc.at[pl.ds(me * per_src, per_src)],
            send_sem=kv_send.at[p],
            recv_sem=kv_recv.at[me],
            device_id=(rank, p),
            device_id_type=MESH,
        )

    def token_copy(src, dst, send, recv, p, j):
        return pltpu.make_async_remote_copy(
            src_ref=src.at[pl.ds(j * BLOCK, BLOCK), pl.ds(pl.multiple_of(p * heads, heads), heads)],
            dst_ref=dst.at[me, j],
            send_sem=send.at[p, j],
            recv_sem=recv.at[me, j],
            device_id=(rank, p),
            device_id_type=MESH,
        )

    def own_copy(src, dst, recv, j):
        return pltpu.make_async_copy(
            src.at[pl.ds(j * BLOCK, BLOCK), pl.ds(pl.multiple_of(me * heads, heads), heads)],
            dst.at[me, j],
            recv.at[me, j],
        )

    far_first = list(range(2, n_head)) + [1]
    for d in far_first:
        kv_copy(peer(d)).start()
    own_kv = pltpu.make_async_copy(
        kv_in.at[me], kv_loc.at[pl.ds(me * per_src, per_src)], kv_recv.at[me]
    )
    own_kv.start()
    for j in range(per_src):
        own_copy(q_hbm, q_buf, q_recv, j).start()
        own_copy(g_hbm, g_buf, g_recv, j).start()
    for j in range(per_src):
        for d in far_first:
            token_copy(q_hbm, q_buf, q_send, q_recv, peer(d), j).start()
            token_copy(g_hbm, g_buf, g_send, g_recv, peer(d), j).start()

    own_kv.wait()
    for d in range(1, n_head):
        p = peer(d)
        kv_here = kv_loc.at[pl.ds(p * per_src, per_src)]
        pltpu.make_async_copy(kv_here, kv_here, kv_recv.at[p]).wait()

    first = rank * blocks

    def wanted_by(s):
        best = jnp.where(rank + 1 == s, blocks - 1, 0)
        for i in range(blocks):
            at = s * blocks + i
            for j in range(3, n_slot):
                local = pair_tab[j, at] - first
                named = (kind_tab[j, at] > 0) & (local >= 0) & (local < blocks)
                best = jnp.where(named, jnp.maximum(best, local), best)
        return best

    def arr_copy(s):
        return pltpu.make_async_remote_copy(
            src_ref=outgoing.at[s],
            dst_ref=arrived.at[rank],
            send_sem=arr_send.at[s],
            recv_sem=arr_recv.at[rank],
            device_id=(s, me),
            device_id_type=MESH,
        )

    def send_block(s, c):
        outgoing[s] = kv_loc[wanted_by(s)]
        arr_copy(s).start()
        return c

    lax.fori_loop(rank + 1, n_ctx, send_block, 0)
    arrived[rank] = kv_loc[0]

    spread = (
        lax.broadcasted_iota(jnp.int32, (BLOCK, lanes), 1) // heads
        == lax.broadcasted_iota(jnp.int32, (BLOCK, lanes), 0)
    ).astype(jnp.float32)
    own_row = lax.broadcasted_iota(jnp.int32, (heads, lanes), 1) % heads == lax.broadcasted_iota(
        jnp.int32, (heads, lanes), 0
    )
    for stat_ref, stat_rows in ((log_ref, log_rows), (delta_ref, delta_rows)):
        for i in range(blocks):
            by_lane = jnp.dot(
                stat_ref[:, i * BLOCK : (i + 1) * BLOCK],
                spread,
                precision=lax.Precision.HIGHEST,
                preferred_element_type=jnp.float32,
            )
            stat_rows[i] = jnp.sum(jnp.where(own_row, by_lane, 0.0), axis=0, keepdims=True)
    acc[...] = jnp.zeros_like(acc)
    acc_hub[...] = jnp.zeros_like(acc_hub)

    def take_block(o, c):
        pltpu.make_async_copy(arrived.at[o], arrived.at[o], arr_recv.at[o]).wait()
        return c

    lax.fori_loop(0, rank, take_block, 0)

    key_row = lax.broadcasted_iota(jnp.int32, (keys, lanes), 0)
    causal = (key_row >= BLOCK) | (
        key_row <= lax.broadcasted_iota(jnp.int32, (keys, lanes), 1) // heads
    )

    def dq_copy(p, j):
        return pltpu.make_async_remote_copy(
            src_ref=dq_buf.at[p, j],
            dst_ref=dq_out.at[
                pl.ds(j * BLOCK, BLOCK), pl.ds(pl.multiple_of(me * heads, heads), heads)
            ],
            send_sem=dq_send.at[p, j],
            recv_sem=dq_recv.at[me, j],
            device_id=(rank, p),
            device_id_type=MESH,
        )

    def own_dq(j):
        return pltpu.make_async_copy(
            dq_buf.at[me, j],
            dq_out.at[pl.ds(j * BLOCK, BLOCK), pl.ds(pl.multiple_of(me * heads, heads), heads)],
            dq_recv.at[me, j],
        )

    def far_owner(i, j):
        at = first + i
        return jnp.where(kind_tab[j, at] > 0, lax.div(pair_tab[j, at], blocks), rank)

    def block_step(t, c):
        d = t // (2 * per_src) * 2 + lax.rem(t, 2)
        j = lax.rem(t // 2, per_src)
        p = peer(d)
        i = p * per_src + j
        pltpu.make_async_copy(q_buf.at[p, j], q_buf.at[p, j], q_recv.at[p, j]).wait()
        pltpu.make_async_copy(g_buf.at[p, j], g_buf.at[p, j], g_recv.at[p, j]).wait()
        kcat[0:BLOCK] = kv_loc[i]
        kcat[BLOCK : 2 * BLOCK] = jnp.where(
            i == 0,
            arrived[jnp.maximum(rank - 1, 0)],
            kv_loc[jnp.maximum(i - 1, 0)],
        )
        kcat[2 * BLOCK : 3 * BLOCK] = arrived[0]
        for slot in range(3, n_slot):
            kcat[slot * BLOCK : (slot + 1) * BLOCK] = arrived[far_owner(i, slot)]
        key_tile = kcat[:, :width]
        value_tile = kcat[:, width:]
        q = q_buf[p, j].astype(jnp.float32).reshape(lanes, width).astype(jnp.bfloat16)
        g = g_buf[p, j].astype(jnp.float32).reshape(lanes, width).astype(jnp.bfloat16)
        nt = (((1,), (1,)), ((), ()))
        scores = lax.dot_general(key_tile, q, nt, preferred_element_type=jnp.float32) * scale
        weights = jnp.exp(scores - log_rows[i])
        slot_mask = jnp.ones((keys, 1), jnp.int32)
        slot_row = lax.broadcasted_iota(jnp.int32, (keys, 1), 0) // BLOCK
        for slot in range(1, n_slot):
            kind = kind_tab[slot, first + i]
            slot_mask = jnp.where(slot_row == slot, kind, slot_mask)
        weights = jnp.where(causal & (slot_mask > 0), weights, 0.0)
        rounded = weights.astype(jnp.bfloat16)
        prob_grad = lax.dot_general(value_tile, g, nt, preferred_element_type=jnp.float32)
        dscore = (weights * (prob_grad - delta_rows[i])).astype(jnp.bfloat16)
        dv = jnp.dot(rounded, g, preferred_element_type=jnp.float32)
        dk = jnp.dot(dscore, q, preferred_element_type=jnp.float32)
        dq = lax.dot_general(
            dscore, key_tile, (((0,), (0,)), ((), ())), preferred_element_type=jnp.float32
        )
        dq_buf[p, j] = (dq * scale).reshape(BLOCK, heads, width).astype(jnp.bfloat16)

        @pl.when(d == 0)
        def _():
            own_dq(j).start()

        @pl.when(d > 0)
        def _():
            dq_copy(p, j).start()

        for u, terms in enumerate((dk, dv)):
            acc[u, i + 1] += terms[:BLOCK]
            acc[u, i] += terms[BLOCK : 2 * BLOCK]
            acc_hub[u] += terms[2 * BLOCK : 3 * BLOCK]
            for slot in range(3, n_slot):
                far_terms[u, i, slot - 3] = terms[slot * BLOCK : (slot + 1) * BLOCK]
        return c

    lax.fori_loop(0, blocks, block_step, 0)

    def ret_copy(u, o):
        return pltpu.make_async_remote_copy(
            src_ref=part.at[u, o],
            dst_ref=ret.at[u, rank],
            send_sem=ret_send.at[u, o],
            recv_sem=ret_recv.at[u, rank],
            device_id=(o, me),
            device_id_type=MESH,
        )

    def send_part(u, o):
        terms = jnp.where(o == 0, acc_hub[u], 0.0) + jnp.where(o == rank - 1, acc[u, 0], 0.0)
        for i in range(blocks):
            for slot in range(3, n_slot):
                terms += jnp.where(far_owner(i, slot) == o, far_terms[u, i, slot - 3], 0.0)
        part[u, o] = terms
        ret_copy(u, o).start()

    def take_part(u, s):
        pltpu.make_async_copy(ret.at[u, s], ret.at[u, s], ret_recv.at[u, s]).wait()
        b = wanted_by(s)
        for i in range(blocks):
            acc[u, i + 1] += jnp.where(b == i, ret[u, s], 0.0)

    def fin_copy(u, p):
        return pltpu.make_async_remote_copy(
            src_ref=fin.at[u, p],
            dst_ref=(dk_land, dv_land)[u].at[me],
            send_sem=fin_send.at[u, p],
            recv_sem=fin_recv.at[u, me],
            device_id=(rank, p),
            device_id_type=MESH,
        )

    def own_fin(u):
        return pltpu.make_async_copy(
            fin.at[u, me], (dk_land, dv_land)[u].at[me], fin_recv.at[u, me]
        )

    def each(step, u):
        def body(k, c):
            step(u, k)
            return c

        return body

    for u in range(2):
        lax.fori_loop(0, rank, each(send_part, u), 0)
    for u in range(2):
        acc[u, 1] += jnp.where(rank == 0, acc_hub[u], 0.0)
        lax.fori_loop(rank + 1, n_ctx, each(take_part, u), 0)
        for i in range(blocks):
            fin[u, i // per_src, i % per_src] = (
                acc[u, i + 1] * scale if u == 0 else acc[u, i + 1]
            ).astype(jnp.bfloat16)
        for d in far_first:
            fin_copy(u, peer(d)).start()
        own_fin(u).start()

    def take_fin(u, land):
        own_fin(u).wait()
        for d in range(1, n_head):
            p = peer(d)
            pltpu.make_async_copy(land.at[p], land.at[p], fin_recv.at[u, p]).wait()

    take_fin(0, dk_land)
    dk_out[...] = by_token(dk_land, wide)

    def sent_block(s, c):
        arr_copy(s).wait_send()
        return c

    lax.fori_loop(rank + 1, n_ctx, sent_block, 0)

    def sent_part(o, c):
        ret_copy(0, o).wait_send()
        ret_copy(1, o).wait_send()
        return c

    lax.fori_loop(0, rank, sent_part, 0)
    for d in range(1, n_head):
        p = peer(d)
        kv_copy(p).wait_send()
        for j in range(per_src):
            token_copy(q_hbm, q_buf, q_send, q_recv, p, j).wait_send()
            token_copy(g_hbm, g_buf, g_send, g_recv, p, j).wait_send()
            dq_copy(p, j).wait_send()
            dq_here = dq_out.at[
                pl.ds(j * BLOCK, BLOCK), pl.ds(pl.multiple_of(p * heads, heads), heads)
            ]
            pltpu.make_async_copy(dq_here, dq_here, dq_recv.at[p, j]).wait()
        for u in range(2):
            fin_copy(u, p).wait_send()
    for j in range(per_src):
        own_dq(j).wait()
    take_fin(1, dv_land)


def by_token(land, wide):
    n_head, per_src, block, width = land.shape
    rows = per_src * block
    for h in range(n_head):
        wide[pl.ds(h, rows, stride=n_head), :] = (
            land[h].astype(jnp.float32).reshape(rows, width)
        )
    return wide[...].astype(land.dtype)


def tail(
    dq_in, dk_in, dv_in, dq_out, dk_out, dv_out, dq_held, dk_held, dv_land, dv_held, wide, loads, stores
):
    pieces = loads.shape[0] - 2
    step = dq_held.shape[0] // pieces
    parts = [pl.ds(k * step, step) for k in range(pieces)]
    load_dv = pltpu.make_async_copy(dv_in, dv_land, loads.at[pieces + 1])
    store_dv = pltpu.make_async_copy(dv_held, dv_out, stores.at[pieces + 1])
    routes = [(dq_in.at[at], dq_held.at[at], dq_out.at[at]) for at in parts]
    routes.append((dk_in, dk_held, dk_out))
    load_dv.start()
    for k, (source, held, _) in enumerate(routes):
        pltpu.make_async_copy(source, held, loads.at[k]).start()
    load_dv.wait()
    dv_held[...] = by_token(dv_land, wide)
    store_dv.start()
    for k, (source, held, target) in enumerate(routes):
        pltpu.make_async_copy(source, held, loads.at[k]).wait()
        pltpu.make_async_copy(held, target, stores.at[k]).start()
    for k, (_, held, target) in enumerate(routes):
        pltpu.make_async_copy(held, target, stores.at[k]).wait()
    store_dv.wait()


def shards(
    n_ctx,
    n_head,
    queries,
    key_states,
    value_states,
    out_grad,
    log_sums,
    row_deltas,
    block_pairs,
    pair_kinds,
):
    rows, all_heads, width = queries.shape
    heads = all_heads // n_head
    n_slot = block_pairs.shape[1]
    per_src = rows // BLOCK
    blocks = per_src * n_head
    lanes = BLOCK * heads
    bf16, f32 = jnp.bfloat16, jnp.float32
    half = (n_head, per_src, BLOCK, width)
    flat = (rows * n_head, width)
    vmem = pl.BlockSpec(memory_space=pltpu.VMEM)
    anywhere = pl.BlockSpec(memory_space=pl.ANY)
    dma = pltpu.SemaphoreType.DMA
    dq, dk, dv = pl.pallas_call(
        partial(kernel, n_ctx, n_head, n_slot),
        out_shape=(
            jax.ShapeDtypeStruct(queries.shape, bf16),
            jax.ShapeDtypeStruct(flat, bf16),
            jax.ShapeDtypeStruct(half, bf16),
        ),
        in_specs=[
            pl.BlockSpec(memory_space=pltpu.SMEM),
            pl.BlockSpec(memory_space=pltpu.SMEM),
            anywhere,
            anywhere,
            vmem,
            vmem,
            vmem,
            vmem,
        ],
        out_specs=(anywhere, vmem, vmem),
        scratch_shapes=[
            pltpu.VMEM(flat, f32),
            pltpu.VMEM((n_head, per_src, BLOCK, 2 * width), bf16),
            pltpu.VMEM((n_head, per_src, BLOCK, heads, width), bf16),
            pltpu.VMEM((n_head, per_src, BLOCK, heads, width), bf16),
            pltpu.VMEM((blocks, BLOCK, 2 * width), bf16),
            pltpu.VMEM((n_ctx, BLOCK, 2 * width), bf16),
            pltpu.VMEM((n_ctx, BLOCK, 2 * width), bf16),
            pltpu.VMEM((n_slot * BLOCK, 2 * width), bf16),
            pltpu.VMEM((blocks, 1, lanes), f32),
            pltpu.VMEM((blocks, 1, lanes), f32),
            pltpu.VMEM((2, blocks + 1, BLOCK, width), f32),
            pltpu.VMEM((2, BLOCK, width), f32),
            pltpu.VMEM((2, blocks, n_slot - 3, BLOCK, width), f32),
            pltpu.VMEM((n_head, per_src, BLOCK, heads, width), bf16),
            pltpu.VMEM((2, n_ctx, BLOCK, width), f32),
            pltpu.VMEM((2, n_ctx, BLOCK, width), f32),
            pltpu.VMEM((2,) + half, bf16),
            pltpu.VMEM(half, bf16),
            dma((n_head,)),
            dma((n_head,)),
            dma((n_head, per_src)),
            dma((n_head, per_src)),
            dma((n_head, per_src)),
            dma((n_head, per_src)),
            dma((n_ctx,)),
            dma((n_ctx,)),
            dma((n_head, per_src)),
            dma((n_head, per_src)),
            dma((2, n_ctx)),
            dma((2, n_ctx)),
            dma((2, n_head)),
            dma((2, n_head)),
        ],
        compiler_params=pltpu.CompilerParams(
            collective_id=0, has_side_effects=True, vmem_limit_bytes=60 * 1024 * 1024
        ),
    )(
        block_pairs.T,
        pair_kinds.T,
        queries,
        out_grad,
        key_states.reshape(flat),
        value_states.reshape(flat),
        log_sums,
        row_deltas,
    )
    dq, dk, dv = pl.pallas_call(
        tail,
        out_shape=(
            jax.ShapeDtypeStruct(queries.shape, bf16),
            jax.ShapeDtypeStruct(flat, bf16),
            jax.ShapeDtypeStruct(flat, bf16),
        ),
        in_specs=[anywhere] * 3,
        out_specs=(anywhere,) * 3,
        scratch_shapes=[
            pltpu.VMEM(queries.shape, bf16),
            pltpu.VMEM(flat, bf16),
            pltpu.VMEM(half, bf16),
            pltpu.VMEM(flat, bf16),
            pltpu.VMEM(flat, f32),
            dma((6,)),
            dma((6,)),
        ],
    )(dq, dk, dv)
    return dq, dk.reshape(key_states.shape), dv.reshape(value_states.shape)


def solution(mesh):
    tokens = P(("ctx", "head"), None, None)
    stats = P("head", "ctx")
    return jax.shard_map(
        partial(shards, mesh.shape["ctx"], mesh.shape["head"]),
        mesh=mesh,
        in_specs=(tokens, tokens, tokens, tokens, stats, stats, P(), P()),
        out_specs=(tokens, tokens, tokens),
        check_vma=False,
    )
```
